32 devices in a mesh: seq: 8 (over y, x, core), chan: 4 (over z).
Axes of the slice: x: 2, y: 2, z: 4, core: 2. Of those that a mesh axis runs over, the one named last changes fastest.
Arguments:
- layer_input: bfloat16 [4096, 4096], P('chan', 'seq'), may hold values from -6 to 6
- query_proj: bfloat16 [4096, 4096], P('chan', 'seq'), may hold values from -6 to 6
- key_proj: bfloat16 [4096, 4096], P('chan', 'seq'), may hold values from -6 to 6
- value_proj: bfloat16 [4096, 4096], P('chan', 'seq'), may hold values from -6 to 6
- filter_taps: float32 [8, 4096], P('chan', 'seq'), may hold values from -1 to 1
- grad_out: bfloat16 [4096, 4096], P('chan', 'seq'), may hold values from -6 to 6
Outputs:
- mixed_out: bfloat16 [4096, 4096], P('chan', 'seq')
- grad_query: bfloat16 [4096, 4096], P('chan', 'seq')
- grad_key: bfloat16 [4096, 4096], P('chan', 'seq')
- grad_value: bfloat16 [4096, 4096], P('chan', 'seq')
- filter_grad: float32 [8, 4096], P('chan', 'seq')
- weight_grad: float32 [4096, 4096], P('seq', 'chan')
The draws below stay inside these ranges and needn't reach their ends.
All inputs are finite; a program needn't handle non-finite values.
Results may differ from the reference program's by a relative error of at most 0.0058.
Values may be sent and summed in bfloat16 or wider, within the bound.
No kernel may reach another device: no remote copies, remote signals or barrier semaphores. Data moves between devices by JAX's collectives and lax.ppermute only.
A program may use at most 128 MiB of HBM per device.

```python
import math
import jax
import jax.numpy as jnp
from jax import lax

D = 4096
GROUP = 512
LENGTH = 4096
GROUPS = 8


def draw_filter_taps(key, part):
    first_key, second_key = jax.random.split(jax.random.fold_in(key, 7))
    positions = jnp.arange(LENGTH, dtype=jnp.int32).astype(jnp.float32)
    envelope = 0.45 / jnp.sqrt(positions + 8.0)
    noise = jnp.clip(jax.random.normal(first_key, (GROUPS, LENGTH), jnp.float32), -4.0, 4.0)
    gains = jax.random.uniform(second_key, (GROUPS, 1), jnp.float32, 0.7, 1.4)
    return gains * envelope[None, :] * noise


def strengthened(result, own_key, source, target, shards_of, factor):
    owner, partner = [(jnp.arange(result.shape[position]) // (result.shape[position] // shards_of)).reshape([-1 if axis == position else 1 for axis in range(result.ndim)]) for position in (source, target)]
    chosen = jax.random.permutation(own_key, shards_of)[partner]
    strong = (owner == chosen) | (owner == (partner + shards_of // 2) % shards_of)
    return jnp.where(strong, factor * result, result)


def steps_of(stream_key, dims, shards, least, largest):
    level, own = 1.0, jax.random.fold_in(stream_key, 6)
    for dim, blocks in shards:
        steps = jnp.exp(jax.random.uniform(jax.random.fold_in(own, dim), (blocks,), jnp.float32, least / len(shards), largest / len(shards)))
        level = level * jnp.repeat(steps, dims[dim] // blocks).reshape([-1 if axis == dim else 1 for axis in range(len(dims))])
    return level


def normal_values(key, shape, width, most, cuts=(), kind=jnp.bfloat16):
    drawn = width * jax.random.normal(key, shape, jnp.float32)
    if cuts:
        drawn = drawn * steps_of(key, shape, cuts, -0.22, 0.18)
    return jnp.clip(drawn, -most, most).astype(kind)


def noise_with(key, dims, deviation, bound, shards, heavy, kind=jnp.bfloat16):
    drawn = deviation * jax.random.normal(key, dims, jnp.float32)
    if shards:
        drawn = drawn * steps_of(key, dims, shards, -0.22, 0.18)
    return jnp.clip(strengthened(drawn, jax.random.fold_in(key, 3), *heavy), -bound, bound).astype(kind)


def setup_inputs(seed: int = 0) -> dict:
    arg_keys = jax.random.split(jax.random.key(seed), 7)
    layer_input = noise_with(arg_keys[0], (D, LENGTH), 1.0, 6.0, ((0, 4), (1, 8)), (1, 0, 8, 2.0))
    query_proj = normal_values(arg_keys[1], (D, LENGTH), 1.0, 6.0, ((0, 4), (1, 8)))
    key_proj = normal_values(arg_keys[2], (D, LENGTH), 1.0, 6.0, ((0, 4), (1, 8)))
    value_proj = normal_values(arg_keys[3], (D, LENGTH), 1.0, 6.0, ((0, 4), (1, 8)))
    filter_taps = draw_filter_taps(jax.random.fold_in(arg_keys[6], 71), 0)
    grad_out = normal_values(arg_keys[5], (D, LENGTH), 1.0, 6.0, ((0, 4), (1, 8)))
    return {"layer_input": layer_input, "query_proj": query_proj, "key_proj": key_proj, "value_proj": value_proj, "filter_taps": filter_taps, "grad_out": grad_out}


def group_terms(group_block):
    query_rows, key_rows, value_rows, grad_rows, taps = group_block
    float_type = jnp.float32
    mixed_in = (key_rows.astype(float_type) * value_rows.astype(float_type)).astype(jnp.bfloat16)
    upstream = (grad_rows.astype(float_type) * query_rows.astype(float_type)).astype(jnp.bfloat16)
    padded = 2 * LENGTH
    spectrum_in = jnp.fft.rfft(mixed_in.astype(float_type), n=padded, axis=1)
    spectrum_up = jnp.fft.rfft(upstream.astype(float_type), n=padded, axis=1)
    spectrum_taps = jnp.fft.rfft(taps, n=padded)
    conv_out = jnp.fft.irfft(spectrum_in * spectrum_taps[None, :], n=padded, axis=1)[:, :LENGTH]
    conv_out = conv_out.astype(jnp.bfloat16)
    grad_mixed = jnp.fft.irfft(spectrum_up * jnp.conj(spectrum_taps)[None, :], n=padded, axis=1)[:, :LENGTH]
    grad_mixed = grad_mixed.astype(jnp.bfloat16)
    taps_grad = jnp.fft.irfft(lax.optimization_barrier(jnp.sum(spectrum_up * jnp.conj(spectrum_in), axis=0)), n=padded)[:LENGTH]
    taps_grad = taps_grad * (1.0 / math.sqrt(GROUP * LENGTH))
    conv_float = conv_out.astype(float_type)
    grad_float = grad_mixed.astype(float_type)
    mixed_out = (query_rows.astype(float_type) * conv_float).astype(jnp.bfloat16)
    grad_query = (grad_rows.astype(float_type) * conv_float).astype(jnp.bfloat16)
    grad_key = (grad_float * value_rows.astype(float_type)).astype(jnp.bfloat16)
    grad_value = (grad_float * key_rows.astype(float_type)).astype(jnp.bfloat16)
    return (mixed_out, grad_query, grad_key, grad_value, taps_grad)

def reference(layer_input, query_proj, key_proj, value_proj, filter_taps, grad_out):
    groups = D // GROUP
    shaped = (query_proj.reshape(groups, GROUP, LENGTH), key_proj.reshape(groups, GROUP, LENGTH), value_proj.reshape(groups, GROUP, LENGTH), grad_out.reshape(groups, GROUP, LENGTH), filter_taps)
    mixed_out, grad_query, grad_key, grad_value, filter_grad = lax.map(group_terms, shaped)
    mixed_out = mixed_out.reshape(D, LENGTH)
    grad_query = grad_query.reshape(D, LENGTH)
    grad_key = grad_key.reshape(D, LENGTH)
    grad_value = grad_value.reshape(D, LENGTH)
    weight_grad = jnp.dot(layer_input, grad_query.T, preferred_element_type=jnp.float32)
    weight_grad = weight_grad * (1.0 / math.sqrt(LENGTH))
    return (mixed_out, grad_query, grad_key, grad_value, filter_grad, weight_grad)
```

```python
import functools
import math

import jax
import jax.numpy as jnp
from jax import lax
from jax.experimental import pallas as pl
from jax.experimental.pallas import tpu as pltpu
from jax.sharding import PartitionSpec as P

F32 = jnp.float32
BF16 = jnp.bfloat16
EXTRA = 16
CHUNKS = 2


def vmem():
    return pl.BlockSpec(memory_space=pltpu.VMEM)


def smem():
    return pl.BlockSpec(memory_space=pltpu.SMEM)


def call(body, outs, scratch, flops, moved, limit_mib, name, *args):
    many = len(outs) > 1
    specs = [smem()] + [vmem()] * (len(args) - 1)
    got = pl.pallas_call(
        body,
        out_shape=tuple(outs) if many else outs[0],
        in_specs=specs,
        out_specs=tuple([vmem()] * len(outs)) if many else vmem(),
        scratch_shapes=scratch,
        cost_estimate=pl.CostEstimate(
            flops=int(flops), bytes_accessed=int(moved), transcendentals=0
        ),
        compiler_params=pltpu.CompilerParams(vmem_limit_bytes=limit_mib << 20),
        name=name,
    )(*args)
    return got if many else (got,)


def struct(shape, dtype):
    return jax.ShapeDtypeStruct(shape, dtype)


def dot_nn(a, b):
    return lax.dot_general(a, b, (((1,), (0,)), ((), ())), preferred_element_type=F32)


def dot_nt(a, b):
    return lax.dot_general(a, b, (((1,), (1,)), ((), ())), preferred_element_type=F32)


def exchange_slots(pieces, axis):
    count = len(pieces)
    got = [pieces[0]]
    for k in range(1, count):
        got.append(lax.ppermute(pieces[k], axis, [(i, i ^ k) for i in range(count)]))
    return got


def mixed_body(count, piece, group, ids, key, value, taps, *outs):
    me = ids[0]
    for k in range(count):
        dest = me ^ k
        rows = pl.ds(pl.multiple_of(dest * piece, piece), piece)
        outs[k][0:piece, :] = (key[rows, :].astype(F32) * value[rows, :].astype(F32)).astype(BF16)
        row = taps[pl.ds(dest * piece // group, 1), :]
        outs[k][piece : piece + EXTRA, :] = jnp.broadcast_to(row, (EXTRA, row.shape[1])).astype(BF16)


def upstream_body(count, piece, ids, grad, query, *outs):
    me = ids[0]
    for k in range(count):
        dest = me ^ k
        rows = pl.ds(pl.multiple_of(dest * piece, piece), piece)
        outs[k][...] = (grad[rows, :].astype(F32) * query[rows, :].astype(F32)).astype(BF16)


def conv_body(count, piece, ids, *refs):
    me = ids[0]
    slots = refs[:count]
    outs = refs[count : 2 * count]
    toep = refs[2 * count]
    stacked, taps, acc, before = refs[2 * count + 1 :]
    block = stacked.shape[1]
    for k in range(count):
        pos = me ^ k
        stacked[pl.ds(pl.multiple_of(pos * piece, piece), piece), :] = slots[k][0:piece, :]
        taps[pos] = slots[k][piece : piece + 8, :].astype(F32)
    row_id = lax.broadcasted_iota(jnp.int32, (block, block), 0)
    col_id = lax.broadcasted_iota(jnp.int32, (block, block), 1)
    before[...] = jnp.zeros_like(before)

    def build(n, carry):
        base = jnp.broadcast_to(taps[n][0:1, :], (block, block))
        turned = pltpu.roll(base, 0, 1, stride=1, stride_axis=0)
        toep[n] = jnp.where(col_id >= row_id, turned, before[...]).astype(BF16)
        before[...] = turned
        return carry

    lax.fori_loop(0, count, build, 0)
    acc[...] = dot_nn(stacked[...], toep[0])
    for n in range(1, count):
        rows = (count - n) * piece
        acc[n * piece :, :] += dot_nn(stacked[0:rows, :], toep[n])
    for k in range(count):
        pos = me ^ k
        outs[k][...] = acc[pl.ds(pl.multiple_of(pos * piece, piece), piece), :].astype(BF16)


def back_body(count, piece, ids, *refs):
    me = ids[0]
    ups = refs[:count]
    slots = refs[count : 2 * count]
    toep = refs[2 * count]
    outs = refs[2 * count + 1 : 3 * count + 1]
    up_all, in_all, acc, before, sums = refs[3 * count + 1 :]
    block = up_all.shape[1]
    for k in range(count):
        pos = me ^ k
        rows = pl.ds(pl.multiple_of(pos * piece, piece), piece)
        up_all[rows, :] = ups[k][...]
        in_all[rows, :] = slots[k][0:piece, :]
    acc[...] = dot_nt(up_all[...], toep[0])
    for n in range(1, count):
        rows = (count - n) * piece
        acc[0:rows, :] += dot_nt(up_all[n * piece :, :], toep[n])
    row_id = lax.broadcasted_iota(jnp.int32, (block, block), 0)
    col_id = lax.broadcasted_iota(jnp.int32, (block, block), 1)
    keep = col_id + row_id >= block - 1
    flip = (col_id + row_id == block - 1).astype(BF16)
    turned_in = dot_nt(flip, in_all[...]).astype(BF16)
    before[...] = jnp.zeros_like(before)
    for n in reversed(range(count)):
        rows = (count - n) * piece
        prod = dot_nn(turned_in[:, 0:rows], up_all[n * piece :, :])
        both = jnp.where(keep, prod, before[...])
        before[...] = prod
        lined = pltpu.roll(both, 1, 1, stride=1, stride_axis=0)
        total = jnp.sum(lined, axis=0, keepdims=True)
        sums[n] = jnp.broadcast_to(total, (8, block))
    for k in range(count):
        pos = me ^ k
        outs[k][0:piece, :] = acc[pl.ds(pl.multiple_of(pos * piece, piece), piece), :].astype(BF16)
        full = sums[pos]
        high = full.astype(BF16)
        low = (full - high.astype(F32)).astype(BF16)
        outs[k][piece : piece + EXTRA, :] = jnp.concatenate([high, low], axis=0)


def query_body(count, piece, ids, *refs):
    me = ids[0]
    slots = refs[:count]
    query, grad, mixed, grad_query = refs[count:]
    for k in range(count):
        pos = me ^ k
        rows = pl.ds(pl.multiple_of(pos * piece, piece), piece)
        conv = slots[k][...].astype(F32)
        mixed[rows, :] = (query[rows, :].astype(F32) * conv).astype(BF16)
        grad_query[rows, :] = (grad[rows, :].astype(F32) * conv).astype(BF16)


def key_body(count, piece, group, factor, ids, *refs):
    me = ids[0]
    slots = refs[:count]
    key, value, grad_key, grad_value, taps_grad = refs[count:]
    row_id = lax.broadcasted_iota(jnp.int32, taps_grad.shape, 0)
    total = jnp.zeros(taps_grad.shape, F32)
    for k in range(count):
        pos = me ^ k
        rows = pl.ds(pl.multiple_of(pos * piece, piece), piece)
        back = slots[k][0:piece, :].astype(F32)
        grad_key[rows, :] = (back * value[rows, :].astype(F32)).astype(BF16)
        grad_value[rows, :] = (back * key[rows, :].astype(F32)).astype(BF16)
        tail = slots[k][piece : piece + EXTRA, :].astype(F32)
        row = tail[0:1, :] + tail[8:9, :]
        total = total + jnp.where(row_id == pos * piece // group, row, 0.0)
    taps_grad[...] = total * factor


def weight_body(chans, ids, own_grad, other_grad, *refs):
    chip, plane = ids[0], ids[1]
    sources = refs[: 2 * chans - 1]
    mine, send_p, send_q, keep_p, keep_q, stack = refs[2 * chans - 1 :]
    rows = sources[0].shape[1]
    half = mine.shape[1] // 2
    for r in range(chans):
        delta = (chip ^ r) - plane
        for step in range(1 - chans, chans):
            source = sources[step] if step >= 0 else sources[chans - 1 - step]

            @pl.when(delta == step)
            def _(source=source, r=r):
                stack[0, r * rows : (r + 1) * rows, :] = source[0]
                stack[1, r * rows : (r + 1) * rows, :] = source[1]

    def part(r, first):
        a = stack[0, r * rows : (r + 1) * rows, :]
        b = stack[1, r * rows : (r + 1) * rows, :]
        cols = slice(first, first + half)
        return dot_nt(a, own_grad[cols, :]) + dot_nt(b, other_grad[cols, :])

    for side in range(2):
        first = side * half
        send = (send_p, send_q)[side]
        order = (1, 3) if side == 0 else (2, 3)
        for n in range(2):
            send[n] = part(order[n], first).astype(BF16)
        (keep_p, keep_q)[side][...] = part(3 - order[0], first)
        mine[:, first : first + half] = part(0, first)


def middle_body(ids, keep_p, got_p, keep_q, got_q, out_p, out_q):
    out_p[...] = (keep_p[...] + got_p[1].astype(F32)).astype(BF16)
    out_q[...] = (keep_q[...] + got_q[1].astype(F32)).astype(BF16)


def finish_body(chunks, factor, ids, *refs):
    out = refs[-1]
    rows = refs[0].shape[0]
    half = refs[0].shape[1] // 2
    for n in range(chunks):
        mine, got_p, got_q, last_p, last_q = refs[5 * n : 5 * n + 5]
        here = slice(n * rows, (n + 1) * rows)
        left = mine[:, :half] + got_p[0].astype(F32) + last_p[...].astype(F32)
        right = mine[:, half:] + got_q[0].astype(F32) + last_q[...].astype(F32)
        out[here, :half] = left * factor
        out[here, half:] = right * factor


def line_gather(block, chans):
    above, below = [block], []
    up, down = block, block
    for step in range(1, chans):
        up = lax.ppermute(up, "chan", [(i, i - 1) for i in range(1, chans) if i + step - 1 < chans])
        down = lax.ppermute(down, "chan", [(i, i + 1) for i in range(chans - 1) if i - step + 1 >= 0])
        above.append(up)
        below.append(down)
    return above + below


def weight_special(layer_input, seq_id, chan_id):
    channels, tok = layer_input.shape
    chans = lax.axis_size("chan")
    half = channels // 2
    core = seq_id % 2
    swap = [(i, i ^ 1) for i in range(lax.axis_size("seq"))]
    give = lax.dynamic_slice_in_dim(layer_input, (1 - core) * half, half, 0)
    keep = lax.dynamic_slice_in_dim(layer_input, core * half, half, 0)
    other = lax.ppermute(give, "seq", swap)
    rows = half // CHUNKS
    gathered = []
    for n in range(CHUNKS):
        here = slice(n * rows, (n + 1) * rows)
        gathered.append(line_gather(jnp.stack([keep[here], other[here]]), chans))
    return gathered


def weight_finish(gathered, grad_query, seq_id, chan_id, factor):
    chans = lax.axis_size("chan")
    seqs = lax.axis_size("seq")
    outputs, tok = grad_query.shape
    half = outputs // 2
    swap = [(i, i ^ 1) for i in range(seqs)]
    along = [(i, i ^ 2) for i in range(seqs)]
    across = [(i, i ^ 4) for i in range(seqs)]
    other_grad = lax.ppermute(grad_query, "seq", swap)
    ids = jnp.stack([seq_id // 2, chan_id])
    parts = []
    for sources in gathered:
        rows = sources[0].shape[1]
        mine, send_p, send_q, keep_p, keep_q = call(
            functools.partial(weight_body, chans),
            [
                struct((rows, outputs), F32),
                struct((2, rows, half), BF16),
                struct((2, rows, half), BF16),
                struct((rows, half), F32),
                struct((rows, half), F32),
            ],
            [pltpu.VMEM((2, chans * rows, tok), BF16)],
            4 * chans * rows * outputs * tok,
            12 << 20,
            32,
            "weight",
            ids,
            grad_query,
            other_grad,
            *sources,
        )
        got_p = lax.ppermute(send_p, "seq", along)
        got_q = lax.ppermute(send_q, "seq", across)
        next_p, next_q = call(
            middle_body,
            [struct((rows, half), BF16)] * 2,
            [],
            rows * outputs,
            4 << 20,
            8,
            "middle",
            ids,
            keep_p,
            got_p,
            keep_q,
            got_q,
        )
        last_p = lax.ppermute(next_p, "seq", across)
        last_q = lax.ppermute(next_q, "seq", along)
        parts += [mine, got_p, got_q, last_p, last_q]
    (out,) = call(
        functools.partial(finish_body, len(gathered), factor),
        [struct((len(gathered) * parts[0].shape[0], outputs), F32)],
        [],
        3 * outputs * outputs,
        8 << 20,
        16,
        "finish",
        ids,
        *parts,
    )
    return out


def weight_general(layer_input, grad_query, factor):
    gathered = lax.all_gather(layer_input, "chan", axis=0, tiled=True)
    summed = lax.psum_scatter(
        jnp.einsum("it,jt->ij", gathered, grad_query, preferred_element_type=F32),
        "seq",
        scatter_dimension=0,
        tiled=True,
    )
    return summed * factor


def per_device(layer_input, query_proj, key_proj, value_proj, filter_taps, grad_out):
    seqs = lax.axis_size("seq")
    chans = lax.axis_size("chan")
    channels, tok = query_proj.shape
    length = seqs * tok
    piece = channels // seqs
    group = channels // filter_taps.shape[0]
    weight_factor = 1.0 / math.sqrt(length)
    taps_factor = 1.0 / math.sqrt(group * length)
    seq_id = lax.axis_index("seq")
    chan_id = lax.axis_index("chan")
    ids = jnp.stack([seq_id, chan_id])
    special = seqs == 2 * chans and chans == 4
    small = struct((piece, tok), BF16)
    large = struct((piece + EXTRA, tok), BF16)
    flat = pltpu.VMEM((channels, tok), BF16)
    wide = pltpu.VMEM((channels, tok), F32)
    square = pltpu.VMEM((tok, tok), F32)
    rows8 = pltpu.VMEM((seqs, 8, tok), F32)
    unit = channels * tok
    work = unit * tok * (seqs + 1)

    mixed = call(
        functools.partial(mixed_body, seqs, piece, group),
        [large] * seqs, [], 3 * unit, 6 * unit, 16, "mixed",
        ids, key_proj, value_proj, filter_taps,
    )
    mixed_slots = exchange_slots(mixed, "seq")
    upstream = call(
        functools.partial(upstream_body, seqs, piece),
        [small] * seqs, [], 3 * unit, 6 * unit, 16, "upstream",
        ids, grad_out, query_proj,
    )
    up_slots = exchange_slots(upstream, "seq")
    if special:
        gathered = weight_special(layer_input, seq_id, chan_id)
    conv = call(
        functools.partial(conv_body, seqs, piece),
        [small] * seqs + [struct((seqs, tok, tok), BF16)],
        [flat, rows8, wide, square],
        work, 16 * unit, 40, "conv",
        ids, *mixed_slots,
    )
    conv_slots = exchange_slots(conv[:seqs], "seq")
    mixed_out, grad_query = call(
        functools.partial(query_body, seqs, piece),
        [struct((channels, tok), BF16)] * 2, [], 4 * unit, 10 * unit, 16, "query",
        ids, *conv_slots, query_proj, grad_out,
    )
    back = call(
        functools.partial(back_body, seqs, piece),
        [large] * seqs,
        [flat, flat, wide, square, rows8],
        2 * work, 20 * unit, 40, "back",
        ids, *up_slots, *mixed_slots, conv[seqs],
    )
    back_slots = exchange_slots(back, "seq")
    grad_key, grad_value, filter_grad = call(
        functools.partial(key_body, seqs, piece, group, taps_factor),
        [struct((channels, tok), BF16)] * 2 + [struct(filter_taps.shape, F32)],
        [], 4 * unit, 10 * unit, 16, "key",
        ids, *back_slots, key_proj, value_proj,
    )
    if special:
        weight_grad = weight_finish(gathered, grad_query, seq_id, chan_id, weight_factor)
    else:
        weight_grad = weight_general(layer_input, grad_query, weight_factor)
    return (mixed_out, grad_query, grad_key, grad_value, filter_grad, weight_grad)


def solution(mesh):
    placed = (P("chan", "seq"),) * 6
    return jax.shard_map(
        per_device,
        mesh=mesh,
        in_specs=placed,
        out_specs=(P("chan", "seq"),) * 5 + (P("seq", "chan"),),
        check_vma=False,
    )
```

```python
import functools
import math

import jax
import jax.numpy as jnp
from jax import lax
from jax.experimental import pallas as pl
from jax.experimental.pallas import tpu as pltpu
from jax.sharding import PartitionSpec as P


F32 = jnp.float32
BF16 = jnp.bfloat16
EXTRA = 16
SHARES = (2, 4, 4)


def vmem():
    return pl.BlockSpec(memory_space=pltpu.VMEM)


def smem():
    return pl.BlockSpec(memory_space=pltpu.SMEM)


def call(body, outs, scratch, flops, moved, limit_mib, *args):
    many = len(outs) > 1
    return run_kernel(body, outs, scratch, flops, moved, limit_mib, many, *args)


def run_kernel(body, outs, scratch, flops, moved, limit_mib, many, *args):
    specs = [smem()] + [vmem()] * (len(args) - 1)
    got = pl.pallas_call(
        body,
        out_shape=tuple(outs) if many else outs[0],
        in_specs=specs,
        out_specs=tuple([vmem()] * len(outs)) if many else vmem(),
        scratch_shapes=scratch,
        cost_estimate=pl.CostEstimate(
            flops=int(flops), bytes_accessed=int(moved), transcendentals=0
        ),
        compiler_params=pltpu.CompilerParams(vmem_limit_bytes=limit_mib << 20),
    )(*args)
    return got if many else (got,)


def struct(shape, dtype):
    return jax.ShapeDtypeStruct(shape, dtype)


def dot_nn(a, b):
    return lax.dot_general(a, b, (((1,), (0,)), ((), ())), preferred_element_type=F32)


def dot_nt(a, b):
    return lax.dot_general(a, b, (((1,), (1,)), ((), ())), preferred_element_type=F32)


def exchange_slots(pieces, axis):
    count = len(pieces)
    got = [pieces[0]]
    for k in range(1, count):
        pairs = [(i, i ^ k) for i in range(count)]
        got.append(lax.ppermute(pieces[k], axis, pairs))
    return got


def mixed_body(count, piece, group, ids, key, value, taps, *outs):
    me = ids[0]
    for k in range(count):
        dest = me ^ k
        rows = pl.ds(pl.multiple_of(dest * piece, piece), piece)
        outs[k][0:piece, :] = (key[rows, :].astype(F32) * value[rows, :].astype(F32)).astype(BF16)
        row = taps[pl.ds(dest * piece // group, 1), :]
        outs[k][piece : piece + EXTRA, :] = jnp.broadcast_to(row, (EXTRA, row.shape[1])).astype(BF16)


def upstream_body(count, piece, ids, grad, query, *outs):
    me = ids[0]
    for k in range(count):
        dest = me ^ k
        rows = pl.ds(pl.multiple_of(dest * piece, piece), piece)
        outs[k][...] = (grad[rows, :].astype(F32) * query[rows, :].astype(F32)).astype(BF16)


def conv_body(count, piece, ids, *refs):
    me = ids[0]
    slots = refs[:count]
    outs = refs[count : 2 * count]
    toep = refs[2 * count]
    stacked, taps, acc, before = refs[2 * count + 1 :]
    block = stacked.shape[1]
    for k in range(count):
        pos = me ^ k
        stacked[pl.ds(pl.multiple_of(pos * piece, piece), piece), :] = slots[k][0:piece, :]
        taps[pos] = slots[k][piece : piece + 8, :].astype(F32)
    row_id = lax.broadcasted_iota(jnp.int32, (block, block), 0)
    col_id = lax.broadcasted_iota(jnp.int32, (block, block), 1)
    before[...] = jnp.zeros_like(before)

    def build(n, carry):
        base = jnp.broadcast_to(taps[n][0:1, :], (block, block))
        turned = pltpu.roll(base, 0, 1, stride=1, stride_axis=0)
        toep[n] = jnp.where(col_id >= row_id, turned, before[...]).astype(BF16)
        before[...] = turned
        return carry

    lax.fori_loop(0, count, build, 0)
    acc[...] = dot_nn(stacked[...], toep[0])
    for n in range(1, count):
        rows = (count - n) * piece
        acc[n * piece :, :] += dot_nn(stacked[0:rows, :], toep[n])
    for k in range(count):
        pos = me ^ k
        outs[k][...] = acc[pl.ds(pl.multiple_of(pos * piece, piece), piece), :].astype(BF16)


def back_body(count, piece, ids, *refs):
    me = ids[0]
    ups = refs[:count]
    slots = refs[count : 2 * count]
    toep = refs[2 * count]
    outs = refs[2 * count + 1 : 3 * count + 1]
    up_all, in_all, acc, before, sums = refs[3 * count + 1 :]
    block = up_all.shape[1]
    for k in range(count):
        pos = me ^ k
        rows = pl.ds(pl.multiple_of(pos * piece, piece), piece)
        up_all[rows, :] = ups[k][...]
        in_all[rows, :] = slots[k][0:piece, :]
    acc[...] = dot_nt(up_all[...], toep[0])
    for n in range(1, count):
        rows = (count - n) * piece
        acc[0:rows, :] += dot_nt(up_all[n * piece :, :], toep[n])
    row_id = lax.broadcasted_iota(jnp.int32, (block, block), 0)
    col_id = lax.broadcasted_iota(jnp.int32, (block, block), 1)
    keep = col_id + row_id >= block - 1
    flip = (col_id + row_id == block - 1).astype(BF16)
    turned_in = dot_nt(flip, in_all[...]).astype(BF16)
    before[...] = jnp.zeros_like(before)
    for n in reversed(range(count)):
        rows = (count - n) * piece
        prod = dot_nn(turned_in[:, 0:rows], up_all[n * piece :, :])
        both = jnp.where(keep, prod, before[...])
        before[...] = prod
        lined = pltpu.roll(both, 1, 1, stride=1, stride_axis=0)
        total = jnp.sum(lined, axis=0, keepdims=True)
        sums[n] = jnp.broadcast_to(total, (8, block))
    for k in range(count):
        pos = me ^ k
        outs[k][0:piece, :] = acc[pl.ds(pl.multiple_of(pos * piece, piece), piece), :].astype(BF16)
        full = sums[pos]
        high = full.astype(BF16)
        low = (full - high.astype(F32)).astype(BF16)
        outs[k][piece : piece + EXTRA, :] = jnp.concatenate([high, low], axis=0)


def query_body(count, piece, ids, *refs):
    me = ids[0]
    slots = refs[:count]
    query, grad, mixed, grad_query = refs[count:]
    for k in range(count):
        pos = me ^ k
        rows = pl.ds(pl.multiple_of(pos * piece, piece), piece)
        conv = slots[k][...].astype(F32)
        mixed[rows, :] = (query[rows, :].astype(F32) * conv).astype(BF16)
        grad_query[rows, :] = (grad[rows, :].astype(F32) * conv).astype(BF16)


def key_body(count, piece, group, factor, ids, *refs):
    me = ids[0]
    slots = refs[:count]
    key, value, grad_key, grad_value, taps_grad = refs[count:]
    row_id = lax.broadcasted_iota(jnp.int32, taps_grad.shape, 0)
    total = jnp.zeros(taps_grad.shape, F32)
    for k in range(count):
        pos = me ^ k
        rows = pl.ds(pl.multiple_of(pos * piece, piece), piece)
        back = slots[k][0:piece, :].astype(F32)
        grad_key[rows, :] = (back * value[rows, :].astype(F32)).astype(BF16)
        grad_value[rows, :] = (back * key[rows, :].astype(F32)).astype(BF16)
        tail = slots[k][piece : piece + EXTRA, :].astype(F32)
        row = tail[0:1, :] + tail[8:9, :]
        total = total + jnp.where(row_id == pos * piece // group, row, 0.0)
    taps_grad[...] = total * factor


def weight_body(chans, ids, own_grad, other_grad, *refs):
    chip, plane = ids[0], ids[1]
    own, a1, a2, a3, b1, b2 = refs[:6]
    mine, send_p, send_q, keep_p, keep_q, stack = refs[6:]
    rows = own.shape[1]
    half = mine.shape[1] // 2
    inner = (plane == 1) | (plane == 2)
    outer = jnp.logical_not(inner)
    for r in range(chans):
        apart = (chip ^ r) ^ plane
        choices = (
            (own, apart == 0),
            (a1, apart == 1),
            (b2, (apart == 2) & inner),
            (a2, (apart == 2) & outer),
            (b1, (apart == 3) & inner),
            (a3, (apart == 3) & outer),
        )
        for source, chosen in choices:

            @pl.when(chosen)
            def _(source=source, r=r):
                stack[0, r * rows : (r + 1) * rows, :] = source[0]
                stack[1, r * rows : (r + 1) * rows, :] = source[1]

    def part(r, first):
        a = stack[0, r * rows : (r + 1) * rows, :]
        b = stack[1, r * rows : (r + 1) * rows, :]
        cols = slice(first, first + half)
        return dot_nt(a, own_grad[cols, :]) + dot_nt(b, other_grad[cols, :])

    for side in range(2):
        first = side * half
        send = (send_p, send_q)[side]
        order = (1, 3) if side == 0 else (2, 3)
        for n in range(2):
            send[n] = part(order[n], first).astype(BF16)
        (keep_p, keep_q)[side][...] = part(3 - order[0], first)
        mine[:, first : first + half] = part(0, first)


def middle_body(ids, keep_p, got_p, keep_q, got_q, out_p, out_q):
    out_p[...] = (keep_p[...] + got_p[1].astype(F32)).astype(BF16)
    out_q[...] = (keep_q[...] + got_q[1].astype(F32)).astype(BF16)


def finish_body(chunks, factor, ids, *refs):
    out = refs[-1]
    half = refs[0].shape[1] // 2
    first = 0
    for n in range(chunks):
        mine, got_p, got_q, last_p, last_q = refs[5 * n : 5 * n + 5]
        here = slice(first, first + mine.shape[0])
        first += mine.shape[0]
        left = mine[:, :half] + got_p[0].astype(F32) + last_p[...].astype(F32)
        right = mine[:, half:] + got_q[0].astype(F32) + last_q[...].astype(F32)
        out[here, :half] = left * factor
        out[here, half:] = right * factor


def plane_pairs(seqs, chans):
    outer = [(i, i ^ 1) for i in range(chans)]
    middle = []
    for i in range(seqs):
        for j in range(chans):
            to = (i, j ^ 3) if j in (1, 2) else (i ^ 1, j)
            middle.append((i * chans + j, to[0] * chans + to[1]))
    return outer, middle


def gather_planes(block, seqs, chans):
    outer, middle = plane_pairs(seqs, chans)
    both = ("seq", "chan")
    a1 = lax.ppermute(block, "chan", outer)
    b1 = lax.ppermute(block, both, middle)
    a2 = lax.ppermute(b1, "chan", outer)
    b2 = lax.ppermute(a1, both, middle)
    a3 = lax.ppermute(b2, "chan", outer)
    return [block, a1, a2, a3, b1, b2]


def weight_start(layer_input, seq_id):
    channels, _ = layer_input.shape
    seqs, chans = lax.axis_size("seq"), lax.axis_size("chan")
    half = channels // 2
    core = seq_id & 1
    swap = [(i, i ^ 1) for i in range(seqs)]
    give = lax.dynamic_slice_in_dim(layer_input, (1 - core) * half, half, 0)
    keep = lax.dynamic_slice_in_dim(layer_input, core * half, half, 0)
    other = lax.ppermute(give, "seq", swap)
    gathered = []
    first = 0
    for share in SHARES:
        here = slice(first, first + half // share)
        first += half // share
        gathered.append(gather_planes(jnp.stack([keep[here], other[here]]), seqs, chans))
    return gathered


def weight_finish(gathered, grad_query, seq_id, chan_id, factor):
    seqs, chans = lax.axis_size("seq"), lax.axis_size("chan")
    outputs, tok = grad_query.shape
    half = outputs // 2
    swap = [(i, i ^ 1) for i in range(seqs)]
    along = [(i, i ^ 2) for i in range(seqs)]
    across = [(i, i ^ 4) for i in range(seqs)]
    other_grad = lax.ppermute(grad_query, "seq", swap)
    ids = jnp.stack([seq_id >> 1, chan_id])
    parts = []
    for sources in gathered:
        rows = sources[0].shape[1]
        mine, send_p, send_q, keep_p, keep_q = call(
            functools.partial(weight_body, chans),
            [
                struct((rows, outputs), F32),
                struct((2, rows, half), BF16),
                struct((2, rows, half), BF16),
                struct((rows, half), F32),
                struct((rows, half), F32),
            ],
            [pltpu.VMEM((2, chans * rows, tok), BF16)],
            4 * chans * rows * outputs * tok,
            12 << 20,
            20,
            ids,
            grad_query,
            other_grad,
            *sources,
        )
        got_p = lax.ppermute(send_p, "seq", along)
        got_q = lax.ppermute(send_q, "seq", across)
        next_p, next_q = call(
            middle_body,
            [struct((rows, half), BF16)] * 2,
            [],
            rows * outputs,
            4 << 20,
            8,
            ids,
            keep_p,
            got_p,
            keep_q,
            got_q,
        )
        last_p = lax.ppermute(next_p, "seq", across)
        last_q = lax.ppermute(next_q, "seq", along)
        parts += [mine, got_p, got_q, last_p, last_q]
    (out,) = call(
        functools.partial(finish_body, len(gathered), factor),
        [struct((channels_of(gathered), outputs), F32)],
        [],
        3 * outputs * outputs,
        8 << 20,
        16,
        ids,
        *parts,
    )
    return out


def channels_of(gathered):
    return sum(sources[0].shape[1] for sources in gathered)


def weight_general(layer_input, grad_query, factor):
    gathered = lax.all_gather(layer_input, "chan", axis=0, tiled=True)
    summed = lax.psum_scatter(
        jnp.einsum("it,jt->ij", gathered, grad_query, preferred_element_type=F32),
        "seq",
        scatter_dimension=0,
        tiled=True,
    )
    return summed * factor


def per_device(layer_input, query_proj, key_proj, value_proj, filter_taps, grad_out):
    seqs = lax.axis_size("seq")
    chans = lax.axis_size("chan")
    channels, tok = query_proj.shape
    length = seqs * tok
    piece = channels // seqs
    group = channels // filter_taps.shape[0]
    weight_factor = 1.0 / math.sqrt(length)
    taps_factor = 1.0 / math.sqrt(group * length)
    seq_id = lax.axis_index("seq")
    chan_id = lax.axis_index("chan")
    ids = jnp.stack([seq_id, chan_id])
    special = seqs == 8 and chans == 4
    small = struct((piece, tok), BF16)
    large = struct((piece + EXTRA, tok), BF16)
    flat = pltpu.VMEM((channels, tok), BF16)
    wide = pltpu.VMEM((channels, tok), F32)
    square = pltpu.VMEM((tok, tok), F32)
    rows8 = pltpu.VMEM((seqs, 8, tok), F32)
    unit = channels * tok
    work = unit * tok * (seqs + 1)

    mixed = call(
        functools.partial(mixed_body, seqs, piece, group),
        [large] * seqs, [], 3 * unit, 6 * unit, 16,
        ids, key_proj, value_proj, filter_taps,
    )
    mixed_slots = exchange_slots(mixed, "seq")
    upstream = call(
        functools.partial(upstream_body, seqs, piece),
        [small] * seqs, [], 3 * unit, 6 * unit, 16,
        ids, grad_out, query_proj,
    )
    up_slots = exchange_slots(upstream, "seq")
    if special:
        gathered = weight_start(layer_input, seq_id)
    conv = call(
        functools.partial(conv_body, seqs, piece),
        [small] * seqs + [struct((seqs, tok, tok), BF16)],
        [flat, rows8, wide, square],
        work, 16 * unit, 22,
        ids, *mixed_slots,
    )
    conv_slots = exchange_slots(conv[:seqs], "seq")
    mixed_out, grad_query = call(
        functools.partial(query_body, seqs, piece),
        [struct((channels, tok), BF16)] * 2, [], 4 * unit, 10 * unit, 16,
        ids, *conv_slots, query_proj, grad_out,
    )
    back = call(
        functools.partial(back_body, seqs, piece),
        [large] * seqs,
        [flat, flat, wide, square, rows8],
        2 * work, 20 * unit, 24,
        ids, *up_slots, *mixed_slots, conv[seqs],
    )
    back_slots = exchange_slots(back, "seq")
    grad_key, grad_value, filter_grad = call(
        functools.partial(key_body, seqs, piece, group, taps_factor),
        [struct((channels, tok), BF16)] * 2 + [struct(filter_taps.shape, F32)],
        [], 4 * unit, 10 * unit, 16,
        ids, *back_slots, key_proj, value_proj,
    )
    if special:
        weight_grad = weight_finish(gathered, grad_query, seq_id, chan_id, weight_factor)
    else:
        weight_grad = weight_general(layer_input, grad_query, weight_factor)
    return (mixed_out, grad_query, grad_key, grad_value, filter_grad, weight_grad)


def solution(mesh):
    placed = (P("chan", "seq"),) * 6
    return jax.shard_map(
        per_device,
        mesh=mesh,
        in_specs=placed,
        out_specs=(P("chan", "seq"),) * 5 + (P("seq", "chan"),),
        check_vma=False,
    )
```

```python
import functools
import math

import jax
import jax.numpy as jnp
from jax import lax
from jax.experimental import pallas as pl
from jax.experimental.pallas import tpu as pltpu
from jax.sharding import PartitionSpec as P


F32 = jnp.float32
BF16 = jnp.bfloat16
EXTRA = 8
QUARTERS = 4


def vmem():
    return pl.BlockSpec(memory_space=pltpu.VMEM)


def call(body, outs, scratch, flops, moved, limit_mib, *args):
    many = len(outs) > 1
    return run_kernel(body, outs, scratch, flops, moved, limit_mib, many, *args)


def run_kernel(body, outs, scratch, flops, moved, limit_mib, many, *args):
    specs = [vmem()] * len(args)
    got = pl.pallas_call(
        body,
        out_shape=tuple(outs) if many else outs[0],
        in_specs=specs,
        out_specs=tuple([vmem()] * len(outs)) if many else vmem(),
        scratch_shapes=scratch,
        cost_estimate=pl.CostEstimate(
            flops=int(flops), bytes_accessed=int(moved), transcendentals=0
        ),
        compiler_params=pltpu.CompilerParams(vmem_limit_bytes=limit_mib << 20),
    )(*args)
    return got if many else (got,)


def struct(shape, dtype):
    return jax.ShapeDtypeStruct(shape, dtype)


def dot_nn(a, b):
    return lax.dot_general(a, b, (((1,), (0,)), ((), ())), preferred_element_type=F32)


def dot_nt(a, b):
    return lax.dot_general(a, b, (((1,), (1,)), ((), ())), preferred_element_type=F32)


def exchange_slots(pieces, axis):
    count = len(pieces)
    got = [pieces[0]]
    for k in range(1, count):
        pairs = [(i, i ^ k) for i in range(count)]
        got.append(lax.ppermute(pieces[k], axis, pairs))
    return got


def mixed_body(count, piece, group, key, value, taps, *outs):
    me = lax.axis_index("seq")
    for k in range(count):
        dest = me ^ k
        rows = pl.ds(pl.multiple_of(dest * piece, piece), piece)
        outs[k][0:piece, :] = (key[rows, :].astype(F32) * value[rows, :].astype(F32)).astype(BF16)
        row = taps[pl.ds(dest * piece // group, 1), :]
        outs[k][piece : piece + EXTRA, :] = jnp.broadcast_to(row, (EXTRA, row.shape[1])).astype(BF16)


def upstream_body(count, piece, grad, query, *outs):
    me = lax.axis_index("seq")
    for k in range(count):
        dest = me ^ k
        rows = pl.ds(pl.multiple_of(dest * piece, piece), piece)
        outs[k][...] = (grad[rows, :].astype(F32) * query[rows, :].astype(F32)).astype(BF16)


def conv_body(count, piece, *refs):
    me = lax.axis_index("seq")
    slots = refs[:count]
    outs = refs[count : 2 * count]
    toep = refs[2 * count]
    stacked, taps, acc, before = refs[2 * count + 1 :]
    block = stacked.shape[1]
    for k in range(count):
        pos = me ^ k
        stacked[pl.ds(pl.multiple_of(pos * piece, piece), piece), :] = slots[k][0:piece, :]
        taps[pos] = slots[k][piece : piece + 8, :].astype(F32)
    row_id = lax.broadcasted_iota(jnp.int32, (block, block), 0)
    col_id = lax.broadcasted_iota(jnp.int32, (block, block), 1)
    before[...] = jnp.zeros_like(before)

    def build(n, carry):
        base = jnp.broadcast_to(taps[n][0:1, :], (block, block))
        turned = pltpu.roll(base, 0, 1, stride=1, stride_axis=0)
        toep[n] = jnp.where(col_id >= row_id, turned, before[...]).astype(BF16)
        before[...] = turned
        return carry

    lax.fori_loop(0, count, build, 0)
    acc[...] = dot_nn(stacked[...], toep[0])
    for n in range(1, count):
        rows = (count - n) * piece
        acc[n * piece :, :] += dot_nn(stacked[0:rows, :], toep[n])
    for k in range(count):
        pos = me ^ k
        outs[k][...] = acc[pl.ds(pl.multiple_of(pos * piece, piece), piece), :].astype(BF16)


def back_body(count, piece, *refs):
    me = lax.axis_index("seq")
    ups = refs[:count]
    slots = refs[count : 2 * count]
    toep = refs[2 * count]
    outs = refs[2 * count + 1 : 3 * count + 1]
    up_all, in_all, acc, before, sums = refs[3 * count + 1 :]
    block = up_all.shape[1]
    for k in range(count):
        pos = me ^ k
        rows = pl.ds(pl.multiple_of(pos * piece, piece), piece)
        up_all[rows, :] = ups[k][...]
        in_all[rows, :] = slots[k][0:piece, :]
    acc[...] = dot_nt(up_all[...], toep[0])
    for n in range(1, count):
        rows = (count - n) * piece
        acc[0:rows, :] += dot_nt(up_all[n * piece :, :], toep[n])
    row_id = lax.broadcasted_iota(jnp.int32, (block, block), 0)
    col_id = lax.broadcasted_iota(jnp.int32, (block, block), 1)
    keep = col_id + row_id >= block - 1
    top = lax.broadcasted_iota(jnp.int32, (EXTRA, block), 0) < EXTRA // 2
    flip = (col_id + row_id == block - 1).astype(BF16)
    turned_in = dot_nt(flip, in_all[...]).astype(BF16)
    before[...] = jnp.zeros_like(before)
    for n in reversed(range(count)):
        rows = (count - n) * piece
        prod = dot_nn(turned_in[:, 0:rows], up_all[n * piece :, :])
        both = jnp.where(keep, prod, before[...])
        before[...] = prod
        lined = pltpu.roll(both, 1, 1, stride=1, stride_axis=0)
        total = jnp.sum(lined, axis=0, keepdims=True)
        sums[n] = jnp.broadcast_to(total, (8, block))
    for k in range(count):
        pos = me ^ k
        outs[k][0:piece, :] = acc[pl.ds(pl.multiple_of(pos * piece, piece), piece), :].astype(BF16)
        full = sums[pos]
        high = full.astype(BF16)
        low = full - high.astype(F32)
        outs[k][piece : piece + EXTRA, :] = jnp.where(top, high.astype(F32), low).astype(BF16)


def query_body(count, piece, *refs):
    me = lax.axis_index("seq")
    slots = refs[:count]
    query, grad, mixed, grad_query = refs[count:]
    for k in range(count):
        pos = me ^ k
        rows = pl.ds(pl.multiple_of(pos * piece, piece), piece)
        conv = slots[k][...].astype(F32)
        mixed[rows, :] = (query[rows, :].astype(F32) * conv).astype(BF16)
        grad_query[rows, :] = (grad[rows, :].astype(F32) * conv).astype(BF16)


def key_body(count, piece, group, factor, *refs):
    me = lax.axis_index("seq")
    slots = refs[:count]
    key, value, grad_key, grad_value, taps_grad = refs[count:]
    row_id = lax.broadcasted_iota(jnp.int32, taps_grad.shape, 0)
    total = jnp.zeros(taps_grad.shape, F32)
    for k in range(count):
        pos = me ^ k
        rows = pl.ds(pl.multiple_of(pos * piece, piece), piece)
        back = slots[k][0:piece, :].astype(F32)
        grad_key[rows, :] = (back * value[rows, :].astype(F32)).astype(BF16)
        grad_value[rows, :] = (back * key[rows, :].astype(F32)).astype(BF16)
        tail = slots[k][piece : piece + EXTRA, :].astype(F32)
        row = tail[0:1, :] + tail[EXTRA // 2 : EXTRA // 2 + 1, :]
        total = total + jnp.where(row_id == pos * piece // group, row, 0.0)
    taps_grad[...] = total * factor


def stack_body(block, other, *outs):
    rows = outs[0].shape[2]
    first = (lax.axis_index("seq") & 1) * block.shape[0] // 2
    for n in range(QUARTERS):
        here = pl.ds(pl.multiple_of(first + n * rows, rows), rows)
        out = outs[n // 2]
        out[n % 2, 0] = block[here, :]
        out[n % 2, 1] = other[here, :]


def weight_body(chans, start, last, own_grad, other_grad, *refs):
    chip, plane = lax.axis_index("seq") >> 1, lax.axis_index("chan")
    own, a1, a2, a3, b1, b2 = refs[:6]
    mine, send_p, send_q, keep_p, keep_q, stack = refs[6:]
    rows = mine.shape[0]
    unit = own.shape[2]
    half = mine.shape[1] // 2
    inner = (plane == 1) | (plane == 2)
    outer = jnp.logical_not(inner)
    for r in range(chans):
        apart = (chip ^ r) ^ plane
        choices = (
            (own, 0, apart == 0),
            (a1, 0, apart == 1),
            (b2, 0, (apart == 2) & inner),
            (a2, 0, (apart == 2) & outer),
            (b1, 0, (apart == 3) & inner),
            (a3, last, (apart == 3) & outer),
        )
        for source, offset, chosen in choices:

            @pl.when(chosen)
            def _(source=source, offset=offset, r=r):
                for n in range(rows // unit):
                    at = r * rows + n * unit
                    for side in range(2):
                        stack[side, at : at + unit, :] = source[start + n - offset, side]

    for side in range(2):
        cols = slice(side * half, (side + 1) * half)
        full = dot_nt(stack[0], own_grad[cols, :]) + dot_nt(stack[1], other_grad[cols, :])
        parts = [full[r * rows : (r + 1) * rows, :] for r in range(chans)]
        given = (send_p, send_q)[side]
        near = 1 + side
        given[0] = parts[near].astype(BF16)
        given[1] = parts[3].astype(BF16)
        (keep_p, keep_q)[side][...] = parts[3 - near]
        mine[:, cols] = parts[0]


def middle_body(keep_p, got_p, keep_q, got_q, out_p, out_q):
    out_p[...] = (keep_p[...] + got_p[1].astype(F32)).astype(BF16)
    out_q[...] = (keep_q[...] + got_q[1].astype(F32)).astype(BF16)


def finish_body(chunks, factor, *refs):
    out = refs[-1]
    half = refs[0].shape[1] // 2
    first = 0
    for n in range(chunks):
        mine, got_p, got_q, last_p, last_q = refs[5 * n : 5 * n + 5]
        here = slice(first, first + mine.shape[0])
        first += mine.shape[0]
        left = mine[:, :half] + got_p[0].astype(F32) + last_p[...].astype(F32)
        right = mine[:, half:] + got_q[0].astype(F32) + last_q[...].astype(F32)
        out[here, :half] = left * factor
        out[here, half:] = right * factor


def plane_pairs(seqs, chans):
    outer = [(i, i ^ 1) for i in range(chans)]
    middle = []
    for i in range(seqs):
        for j in range(chans):
            to = (i, j ^ 3) if j in (1, 2) else (i ^ 1, j)
            middle.append((i * chans + j, to[0] * chans + to[1]))
    return outer, middle


def weight_start(layer_input):
    channels, tok = layer_input.shape
    seqs, chans = lax.axis_size("seq"), lax.axis_size("chan")
    half = channels // 2
    swap = [(i, i ^ 1) for i in range(seqs)]
    other = lax.ppermute(layer_input, "seq", swap)
    quarter = struct((QUARTERS // 2, 2, half // QUARTERS, tok), BF16)
    own = call(
        stack_body, [quarter] * 2, [], half * tok, 4 * half * tok, 58,
        layer_input, other,
    )
    outer, middle = plane_pairs(seqs, chans)
    both = ("seq", "chan")
    a1x = lax.ppermute(own[0], "chan", outer)
    b1x = lax.ppermute(own[0], both, middle)
    a1y = lax.ppermute(own[1], "chan", outer)
    b1y = lax.ppermute(own[1], both, middle)
    a2x = lax.ppermute(b1x, "chan", outer)
    b2x = lax.ppermute(a1x, both, middle)
    a3x = lax.ppermute(b2x, "chan", outer)
    a2y = lax.ppermute(b1y, "chan", outer)
    b2y = lax.ppermute(a1y, both, middle)
    a3y = lax.ppermute(b2y[0:1], "chan", outer)
    a3z = lax.ppermute(b2y[1:2], "chan", outer)
    return [
        (0, 2, 0, (own[0], a1x, a2x, a3x, b1x, b2x)),
        (0, 1, 0, (own[1], a1y, a2y, a3y, b1y, b2y)),
        (1, 1, 1, (own[1], a1y, a2y, a3z, b1y, b2y)),
    ]


def weight_finish(gathered, grad_query, factor):
    seqs, chans = lax.axis_size("seq"), lax.axis_size("chan")
    outputs, tok = grad_query.shape
    half = outputs // 2
    swap = [(i, i ^ 1) for i in range(seqs)]
    along = [(i, i ^ 2) for i in range(seqs)]
    across = [(i, i ^ 4) for i in range(seqs)]
    other_grad = lax.ppermute(grad_query, "seq", swap)
    parts = []
    for start, count, last, sources in gathered:
        rows = count * sources[0].shape[2]
        mine, send_p, send_q, keep_p, keep_q = call(
            functools.partial(weight_body, chans, start, last),
            [
                struct((rows, outputs), F32),
                struct((2, rows, half), BF16),
                struct((2, rows, half), BF16),
                struct((rows, half), F32),
                struct((rows, half), F32),
            ],
            [pltpu.VMEM((2, chans * rows, tok), BF16)],
            4 * chans * rows * outputs * tok,
            12 << 20,
            20,
            grad_query,
            other_grad,
            *sources,
        )
        got_p = lax.ppermute(send_p, "seq", along)
        got_q = lax.ppermute(send_q, "seq", across)
        next_p, next_q = call(
            middle_body,
            [struct((rows, half), BF16)] * 2,
            [],
            rows * outputs,
            4 << 20,
            8,
            keep_p,
            got_p,
            keep_q,
            got_q,
        )
        last_p = lax.ppermute(next_p, "seq", across)
        last_q = lax.ppermute(next_q, "seq", along)
        parts += [mine, got_p, got_q, last_p, last_q]
    (out,) = call(
        functools.partial(finish_body, len(gathered), factor),
        [struct((QUARTERS * gathered[0][3][0].shape[2], outputs), F32)],
        [],
        3 * outputs * outputs,
        8 << 20,
        16,
        *parts,
    )
    return out


def weight_general(layer_input, grad_query, factor):
    gathered = lax.all_gather(layer_input, "chan", axis=0, tiled=True)
    summed = lax.psum_scatter(
        jnp.einsum("it,jt->ij", gathered, grad_query, preferred_element_type=F32),
        "seq",
        scatter_dimension=0,
        tiled=True,
    )
    return summed * factor


def per_device(layer_input, query_proj, key_proj, value_proj, filter_taps, grad_out):
    seqs = lax.axis_size("seq")
    chans = lax.axis_size("chan")
    channels, tok = query_proj.shape
    length = seqs * tok
    piece = channels // seqs
    group = channels // filter_taps.shape[0]
    weight_factor = 1.0 / math.sqrt(length)
    taps_factor = 1.0 / math.sqrt(group * length)
    special = seqs == 8 and chans == 4
    small = struct((piece, tok), BF16)
    large = struct((piece + EXTRA, tok), BF16)
    flat = pltpu.VMEM((channels, tok), BF16)
    wide = pltpu.VMEM((channels, tok), F32)
    square = pltpu.VMEM((tok, tok), F32)
    rows8 = pltpu.VMEM((seqs, 8, tok), F32)
    unit = channels * tok
    work = unit * tok * (seqs + 1)

    mixed = call(
        functools.partial(mixed_body, seqs, piece, group),
        [large] * seqs, [], 3 * unit, 6 * unit, 58,
        key_proj, value_proj, filter_taps,
    )
    mixed_slots = exchange_slots(mixed, "seq")
    upstream = call(
        functools.partial(upstream_body, seqs, piece),
        [small] * seqs, [], 3 * unit, 6 * unit, 16,
        grad_out, query_proj,
    )
    up_slots = exchange_slots(upstream, "seq")
    if special:
        gathered = weight_start(layer_input)
    conv = call(
        functools.partial(conv_body, seqs, piece),
        [small] * seqs + [struct((seqs, tok, tok), BF16)],
        [flat, rows8, wide, square],
        work, 16 * unit, 22,
        *mixed_slots,
    )
    conv_slots = exchange_slots(conv[:seqs], "seq")
    mixed_out, grad_query = call(
        functools.partial(query_body, seqs, piece),
        [struct((channels, tok), BF16)] * 2, [], 4 * unit, 10 * unit, 16,
        *conv_slots, query_proj, grad_out,
    )
    back = call(
        functools.partial(back_body, seqs, piece),
        [large] * seqs,
        [flat, flat, wide, square, rows8],
        2 * work, 20 * unit, 24,
        *up_slots, *mixed_slots, conv[seqs],
    )
    back_slots = exchange_slots(back, "seq")
    grad_key, grad_value, filter_grad = call(
        functools.partial(key_body, seqs, piece, group, taps_factor),
        [struct((channels, tok), BF16)] * 2 + [struct(filter_taps.shape, F32)],
        [], 4 * unit, 10 * unit, 16,
        *back_slots, key_proj, value_proj,
    )
    if special:
        weight_grad = weight_finish(gathered, grad_query, weight_factor)
    else:
        weight_grad = weight_general(layer_input, grad_query, weight_factor)
    return (mixed_out, grad_query, grad_key, grad_value, filter_grad, weight_grad)


def solution(mesh):
    placed = (P("chan", "seq"),) * 6
    return jax.shard_map(
        per_device,
        mesh=mesh,
        in_specs=placed,
        out_specs=(P("chan", "seq"),) * 5 + (P("seq", "chan"),),
        check_vma=False,
    )
```

```python
import functools
import math

import jax
import jax.numpy as jnp
from jax import lax
from jax.experimental import pallas as pl
from jax.experimental.pallas import tpu as pltpu
from jax.sharding import PartitionSpec as P


F32 = jnp.float32
BF16 = jnp.bfloat16
EXTRA = 8
QUARTERS = 4


def vmem():
    return pl.BlockSpec(memory_space=pltpu.VMEM)


def hbm():
    return pl.BlockSpec(memory_space=pltpu.HBM)


def call(body, outs, scratch, flops, moved, limit_mib, *args, raw=0, raw_out=False, alias=None, free=0):
    many = len(outs) > 1
    return run_kernel(body, outs, scratch, flops, moved, limit_mib, many, args, raw, raw_out, alias, free)


def run_kernel(body, outs, scratch, flops, moved, limit_mib, many, args, raw, raw_out, alias, free):
    specs = [hbm()] * raw + [pl.BlockSpec(memory_space=pl.ANY)] * free
    specs += [vmem()] * (len(args) - raw - free)
    out_spec = hbm() if raw_out else vmem()
    got = pl.pallas_call(
        body,
        out_shape=tuple(outs) if many else outs[0],
        in_specs=specs,
        out_specs=tuple([out_spec] * len(outs)) if many else out_spec,
        input_output_aliases=alias or {},
        scratch_shapes=scratch,
        cost_estimate=pl.CostEstimate(
            flops=int(flops), bytes_accessed=int(moved), transcendentals=0
        ),
        compiler_params=pltpu.CompilerParams(vmem_limit_bytes=limit_mib << 20),
    )(*args)
    return got if many else (got,)


def struct(shape, dtype):
    return jax.ShapeDtypeStruct(shape, dtype)


def dot_nn(a, b):
    return lax.dot_general(a, b, (((1,), (0,)), ((), ())), preferred_element_type=F32)


def dot_nt(a, b):
    return lax.dot_general(a, b, (((1,), (1,)), ((), ())), preferred_element_type=F32)


def exchange_slots(pieces, axis):
    count = len(pieces)
    got = [pieces[0]]
    for k in range(1, count):
        pairs = [(i, i ^ k) for i in range(count)]
        got.append(lax.ppermute(pieces[k], axis, pairs))
    return got


def mixed_body(count, piece, group, key, value, taps, *refs):
    outs = refs[:count]
    key_in, value_in, taps_in, block_out, sems = refs[-5:]
    me = lax.axis_index("seq")
    row_copy = pltpu.make_async_copy(taps, taps_in, sems.at[3 * count])
    row_copy.start()
    copies = []
    for k in range(count):
        rows = pl.ds(pl.multiple_of((me ^ k) * piece, piece), piece)
        pair = (
            pltpu.make_async_copy(key.at[rows, :], key_in.at[k], sems.at[3 * k]),
            pltpu.make_async_copy(value.at[rows, :], value_in.at[k], sems.at[3 * k + 1]),
        )
        for copy in pair:
            copy.start()
        copies.append(pair)
    row_copy.wait()
    for k in range(count):
        for copy in copies[k]:
            copy.wait()
        block_out[k, 0:piece, :] = (key_in[k].astype(F32) * value_in[k].astype(F32)).astype(BF16)
        row = taps_in[pl.ds((me ^ k) * piece // group, 1), :]
        block_out[k, piece : piece + EXTRA, :] = jnp.broadcast_to(row, (EXTRA, row.shape[1])).astype(BF16)
        pltpu.make_async_copy(block_out.at[k], outs[k], sems.at[3 * k + 2]).start()
    for k in range(count):
        pltpu.make_async_copy(block_out.at[k], outs[k], sems.at[3 * k + 2]).wait()


def mixed_keep_body(count, piece, group, key, value, taps, block, *refs):
    outs, keeps = refs[:count], refs[count : count + 2]
    keep_in, keep_sems = refs[-2:]
    rows = keep_in.shape[1]
    first = (lax.axis_index("seq") & 1) * block.shape[0] // 2
    for n in range(QUARTERS):
        here = pl.ds(pl.multiple_of(first + n * rows, rows), rows)
        pltpu.make_async_copy(block.at[here, :], keep_in.at[n], keep_sems.at[2 * n]).start()
    mixed_body(count, piece, group, key, value, taps, *outs, *refs[count + 2 : -2])
    for n in range(QUARTERS):
        here = pl.ds(pl.multiple_of(first + n * rows, rows), rows)
        pltpu.make_async_copy(block.at[here, :], keep_in.at[n], keep_sems.at[2 * n]).wait()
        to = keeps[n // 2].at[n % 2, 0]
        pltpu.make_async_copy(keep_in.at[n], to, keep_sems.at[2 * n + 1]).start()
    for n in range(QUARTERS):
        to = keeps[n // 2].at[n % 2, 0]
        pltpu.make_async_copy(keep_in.at[n], to, keep_sems.at[2 * n + 1]).wait()


def upstream_body(count, piece, grad, query, *outs):
    me = lax.axis_index("seq")
    for k in range(count):
        dest = me ^ k
        rows = pl.ds(pl.multiple_of(dest * piece, piece), piece)
        outs[k][...] = (grad[rows, :].astype(F32) * query[rows, :].astype(F32)).astype(BF16)


def conv_body(count, piece, *refs):
    me = lax.axis_index("seq")
    slots = refs[:count]
    outs = refs[count : 2 * count]
    toep = refs[2 * count]
    stacked, taps, acc, before = refs[2 * count + 1 :]
    block = stacked.shape[1]
    for k in range(count):
        pos = me ^ k
        stacked[pl.ds(pl.multiple_of(pos * piece, piece), piece), :] = slots[k][0:piece, :]
        taps[pos] = slots[k][piece : piece + 8, :].astype(F32)
    row_id = lax.broadcasted_iota(jnp.int32, (block, block), 0)
    col_id = lax.broadcasted_iota(jnp.int32, (block, block), 1)
    before[...] = jnp.zeros_like(before)

    def build(n, carry):
        base = jnp.broadcast_to(taps[n][0:1, :], (block, block))
        turned = pltpu.roll(base, 0, 1, stride=1, stride_axis=0)
        toep[n] = jnp.where(col_id >= row_id, turned, before[...]).astype(BF16)
        before[...] = turned
        return carry

    lax.fori_loop(0, count, build, 0)
    acc[...] = dot_nn(stacked[...], toep[0])
    for n in range(1, count):
        rows = (count - n) * piece
        acc[n * piece :, :] += dot_nn(stacked[0:rows, :], toep[n])
    for k in range(count):
        pos = me ^ k
        outs[k][...] = acc[pl.ds(pl.multiple_of(pos * piece, piece), piece), :].astype(BF16)


def back_body(count, piece, *refs):
    me = lax.axis_index("seq")
    ups = refs[:count]
    slots = refs[count : 2 * count]
    toep = refs[2 * count]
    outs = refs[2 * count + 1 : 3 * count + 1]
    up_all, in_all, acc, before, sums = refs[3 * count + 1 :]
    block = up_all.shape[1]
    for k in range(count):
        pos = me ^ k
        rows = pl.ds(pl.multiple_of(pos * piece, piece), piece)
        up_all[rows, :] = ups[k][...]
        in_all[rows, :] = slots[k][0:piece, :]
    acc[...] = dot_nt(up_all[...], toep[0])
    for n in range(1, count):
        rows = (count - n) * piece
        acc[0:rows, :] += dot_nt(up_all[n * piece :, :], toep[n])
    row_id = lax.broadcasted_iota(jnp.int32, (block, block), 0)
    col_id = lax.broadcasted_iota(jnp.int32, (block, block), 1)
    keep = col_id + row_id >= block - 1
    top = lax.broadcasted_iota(jnp.int32, (EXTRA, block), 0) < EXTRA // 2
    flip = (col_id + row_id == block - 1).astype(BF16)
    turned_in = dot_nt(flip, in_all[...]).astype(BF16)
    before[...] = jnp.zeros_like(before)
    for n in reversed(range(count)):
        rows = (count - n) * piece
        prod = dot_nn(turned_in[:, 0:rows], up_all[n * piece :, :])
        both = jnp.where(keep, prod, before[...])
        before[...] = prod
        lined = pltpu.roll(both, 1, 1, stride=1, stride_axis=0)
        total = jnp.sum(lined, axis=0, keepdims=True)
        sums[n] = jnp.broadcast_to(total, (8, block))
    for k in range(count):
        pos = me ^ k
        outs[k][0:piece, :] = acc[pl.ds(pl.multiple_of(pos * piece, piece), piece), :].astype(BF16)
        full = sums[pos]
        high = full.astype(BF16)
        low = full - high.astype(F32)
        outs[k][piece : piece + EXTRA, :] = jnp.where(top, high.astype(F32), low).astype(BF16)


def query_body(count, piece, *refs):
    me = lax.axis_index("seq")
    slots = refs[:count]
    query, grad, mixed, grad_query, again = refs[count:]
    for k in range(count):
        pos = me ^ k
        rows = pl.ds(pl.multiple_of(pos * piece, piece), piece)
        conv = slots[k][...].astype(F32)
        mixed[rows, :] = (query[rows, :].astype(F32) * conv).astype(BF16)
        value = (grad[rows, :].astype(F32) * conv).astype(BF16)
        grad_query[rows, :] = value
        again[rows, :] = value


def key_body(count, piece, group, factor, *refs):
    me = lax.axis_index("seq")
    slots = refs[:count]
    key, value, grad_key, grad_value, taps_grad = refs[count:]
    row_id = lax.broadcasted_iota(jnp.int32, taps_grad.shape, 0)
    total = jnp.zeros(taps_grad.shape, F32)
    for k in range(count):
        pos = me ^ k
        rows = pl.ds(pl.multiple_of(pos * piece, piece), piece)
        back = slots[k][0:piece, :].astype(F32)
        grad_key[rows, :] = (back * value[rows, :].astype(F32)).astype(BF16)
        grad_value[rows, :] = (back * key[rows, :].astype(F32)).astype(BF16)
        tail = slots[k][piece : piece + EXTRA, :].astype(F32)
        row = tail[0:1, :] + tail[EXTRA // 2 : EXTRA // 2 + 1, :]
        total = total + jnp.where(row_id == pos * piece // group, row, 0.0)
    taps_grad[...] = total * factor


def stack_body(kept_x, kept_y, other, *refs):
    del kept_x, kept_y
    outs, sems = refs[:-1], refs[-1]
    rows = outs[0].shape[2]
    first = (lax.axis_index("seq") & 1) * other.shape[0] // 2
    copies = []
    for n in range(QUARTERS):
        here = pl.ds(pl.multiple_of(first + n * rows, rows), rows)
        to = outs[n // 2].at[n % 2, 1]
        copies.append(pltpu.make_async_copy(other.at[here, :], to, sems.at[n]))
    for copy in copies:
        copy.start()
    for copy in copies:
        copy.wait()


def weight_body(chans, start, last, own_grad, other_grad, *refs):
    chip, plane = lax.axis_index("seq") >> 1, lax.axis_index("chan")
    own, a1, a2, a3, b1, b2 = refs[:6]
    mine, send_p, send_q, keep_p, keep_q, stack = refs[6:]
    rows = mine.shape[0]
    unit = own.shape[2]
    half = mine.shape[1] // 2
    inner = (plane == 1) | (plane == 2)
    outer = jnp.logical_not(inner)
    for r in range(chans):
        apart = (chip ^ r) ^ plane
        choices = (
            (own, 0, apart == 0),
            (a1, 0, apart == 1),
            (b2, 0, (apart == 2) & inner),
            (a2, 0, (apart == 2) & outer),
            (b1, 0, (apart == 3) & inner),
            (a3, last, (apart == 3) & outer),
        )
        for source, offset, chosen in choices:

            @pl.when(chosen)
            def _(source=source, offset=offset, r=r):
                for n in range(rows // unit):
                    at = r * rows + n * unit
                    for side in range(2):
                        stack[side, at : at + unit, :] = source[start + n - offset, side]

    for side in range(2):
        cols = slice(side * half, (side + 1) * half)
        full = dot_nt(stack[0], own_grad[cols, :]) + dot_nt(stack[1], other_grad[cols, :])
        parts = [full[r * rows : (r + 1) * rows, :] for r in range(chans)]
        given = (send_p, send_q)[side]
        near = 1 + side
        given[0] = parts[near].astype(BF16)
        given[1] = parts[3].astype(BF16)
        (keep_p, keep_q)[side][...] = parts[3 - near]
        mine[:, cols] = parts[0]


def middle_body(keep_p, got_p, keep_q, got_q, out_p, out_q):
    out_p[...] = (keep_p[...] + got_p[1].astype(F32)).astype(BF16)
    out_q[...] = (keep_q[...] + got_q[1].astype(F32)).astype(BF16)


def finish_body(chunks, begin, factor, *refs):
    out, block, sem = refs[-3:]
    half = refs[0].shape[1] // 2
    first = 0
    for n in range(chunks):
        mine, got_p, got_q, last_p, last_q = refs[5 * n : 5 * n + 5]
        here = slice(first, first + mine.shape[0])
        first += mine.shape[0]
        left = mine[:, :half] + got_p[0].astype(F32) + last_p[...].astype(F32)
        right = mine[:, half:] + got_q[0].astype(F32) + last_q[...].astype(F32)
        block[here, :half] = left * factor
        block[here, half:] = right * factor
    copy = pltpu.make_async_copy(block, out.at[pl.ds(begin, first), :], sem)
    copy.start()
    copy.wait()


def last_body(chunks, begin, factor, whole, *refs):
    del whole
    finish_body(chunks, begin, factor, *refs)


def plane_pairs(seqs, chans):
    outer = [(i, i ^ 1) for i in range(chans)]
    middle = []
    for i in range(seqs):
        for j in range(chans):
            to = (i, j ^ 3) if j in (1, 2) else (i ^ 1, j)
            middle.append((i * chans + j, to[0] * chans + to[1]))
    return outer, middle


def weight_start(other, kept):
    seqs, chans = lax.axis_size("seq"), lax.axis_size("chan")
    quarter = struct(kept[0].shape, BF16)
    own = call(
        stack_body, [quarter] * 2, [pltpu.SemaphoreType.DMA((QUARTERS,))],
        other.size, 2 * other.size, 8,
        *kept, other, raw=2, free=1, raw_out=True, alias={0: 0, 1: 1},
    )
    outer, middle = plane_pairs(seqs, chans)
    both = ("seq", "chan")
    a1x = lax.ppermute(own[0], "chan", outer)
    b1x = lax.ppermute(own[0], both, middle)
    a1y = lax.ppermute(own[1], "chan", outer)
    b1y = lax.ppermute(own[1], both, middle)
    a2x = lax.ppermute(b1x, "chan", outer)
    b2x = lax.ppermute(a1x, both, middle)
    a3x = lax.ppermute(b2x, "chan", outer)
    a2y = lax.ppermute(b1y, "chan", outer)
    b2y = lax.ppermute(a1y, both, middle)
    a3y = lax.ppermute(b2y[0:1], "chan", outer)
    a3z = lax.ppermute(b2y[1:2], "chan", outer)
    return [
        (0, 2, 0, (own[0], a1x, a2x, a3x, b1x, b2x)),
        (0, 1, 0, (own[1], a1y, a2y, a3y, b1y, b2y)),
        (1, 1, 1, (own[1], a1y, a2y, a3z, b1y, b2y)),
    ]


def weight_finish(gathered, grad_query, factor):
    seqs, chans = lax.axis_size("seq"), lax.axis_size("chan")
    outputs, tok = grad_query.shape
    half = outputs // 2
    swap = [(i, i ^ 1) for i in range(seqs)]
    along = [(i, i ^ 2) for i in range(seqs)]
    across = [(i, i ^ 4) for i in range(seqs)]
    other_grad = lax.ppermute(grad_query, "seq", swap)
    parts = []
    for start, count, last, sources in gathered:
        rows = count * sources[0].shape[2]
        mine, send_p, send_q, keep_p, keep_q = call(
            functools.partial(weight_body, chans, start, last),
            [
                struct((rows, outputs), F32),
                struct((2, rows, half), BF16),
                struct((2, rows, half), BF16),
                struct((rows, half), F32),
                struct((rows, half), F32),
            ],
            [pltpu.VMEM((2, chans * rows, tok), BF16)],
            4 * chans * rows * outputs * tok,
            12 << 20,
            12,
            grad_query,
            other_grad,
            *sources,
        )
        got_p = lax.ppermute(send_p, "seq", along)
        got_q = lax.ppermute(send_q, "seq", across)
        next_p, next_q = call(
            middle_body,
            [struct((rows, half), BF16)] * 2,
            [],
            rows * outputs,
            4 << 20,
            8,
            keep_p,
            got_p,
            keep_q,
            got_q,
        )
        last_p = lax.ppermute(next_p, "seq", across)
        last_q = lax.ppermute(next_q, "seq", along)
        parts += [mine, got_p, got_q, last_p, last_q]
    total = QUARTERS * gathered[0][3][0].shape[2]
    result = struct((total, outputs), F32)
    early = total - parts[-5].shape[0]
    (out,) = call(
        functools.partial(finish_body, len(gathered) - 1, 0, factor),
        [result], [pltpu.VMEM((early, outputs), F32), pltpu.SemaphoreType.DMA],
        3 * early * outputs, 8 * early * outputs, 12,
        *parts[:-5], raw_out=True,
    )
    (out,) = call(
        functools.partial(last_body, 1, early, factor),
        [result], [pltpu.VMEM((total - early, outputs), F32), pltpu.SemaphoreType.DMA],
        3 * outputs * (total - early), 8 * outputs * (total - early), 8,
        out, *parts[-5:], raw=1, raw_out=True, alias={0: 0},
    )
    return out


def weight_general(layer_input, grad_query, factor):
    gathered = lax.all_gather(layer_input, "chan", axis=0, tiled=True)
    summed = lax.psum_scatter(
        jnp.einsum("it,jt->ij", gathered, grad_query, preferred_element_type=F32),
        "seq",
        scatter_dimension=0,
        tiled=True,
    )
    return summed * factor


def per_device(layer_input, query_proj, key_proj, value_proj, filter_taps, grad_out):
    seqs = lax.axis_size("seq")
    chans = lax.axis_size("chan")
    channels, tok = query_proj.shape
    length = seqs * tok
    piece = channels // seqs
    group = channels // filter_taps.shape[0]
    weight_factor = 1.0 / math.sqrt(length)
    taps_factor = 1.0 / math.sqrt(group * length)
    special = seqs == 8 and chans == 4
    small = struct((piece, tok), BF16)
    large = struct((piece + EXTRA, tok), BF16)
    flat = pltpu.VMEM((channels, tok), BF16)
    wide = pltpu.VMEM((channels, tok), F32)
    square = pltpu.VMEM((tok, tok), F32)
    rows8 = pltpu.VMEM((seqs, 8, tok), F32)
    unit = channels * tok
    work = unit * tok * (seqs + 1)

    buffers = [
        pltpu.VMEM((seqs, piece, tok), BF16),
        pltpu.VMEM((seqs, piece, tok), BF16),
        pltpu.VMEM(filter_taps.shape, F32),
        pltpu.VMEM((seqs, piece + EXTRA, tok), BF16),
        pltpu.SemaphoreType.DMA((3 * seqs + 1,)),
    ]
    first_args = (key_proj, value_proj, filter_taps)
    if special:
        other = lax.ppermute(layer_input, "seq", [(i, i ^ 1) for i in range(seqs)])
        rows = channels // 2 // QUARTERS
        first = call(
            functools.partial(mixed_keep_body, seqs, piece, group),
            [large] * seqs + [struct((QUARTERS // 2, 2, rows, tok), BF16)] * 2,
            buffers + [pltpu.VMEM((QUARTERS, rows, tok), BF16), pltpu.SemaphoreType.DMA((2 * QUARTERS,))],
            3 * unit, 8 * unit, 58,
            *first_args, layer_input, raw=4, raw_out=True,
        )
        mixed, kept = first[:seqs], first[seqs:]
    else:
        mixed = call(
            functools.partial(mixed_body, seqs, piece, group),
            [large] * seqs, buffers, 3 * unit, 6 * unit, 58,
            *first_args, raw=3, raw_out=True,
        )
    mixed_slots = exchange_slots(mixed, "seq")
    upstream = call(
        functools.partial(upstream_body, seqs, piece),
        [small] * seqs, [], 3 * unit, 6 * unit, 16,
        grad_out, query_proj,
    )
    up_slots = exchange_slots(upstream, "seq")
    if special:
        gathered = weight_start(other, kept)
    conv = call(
        functools.partial(conv_body, seqs, piece),
        [small] * seqs + [struct((seqs, tok, tok), BF16)],
        [flat, rows8, wide, square],
        work, 16 * unit, 14,
        *mixed_slots,
    )
    conv_slots = exchange_slots(conv[:seqs], "seq")
    mixed_out, grad_query, own_grad = call(
        functools.partial(query_body, seqs, piece),
        [struct((channels, tok), BF16)] * 3, [], 4 * unit, 10 * unit, 16,
        *conv_slots, query_proj, grad_out,
    )
    back = call(
        functools.partial(back_body, seqs, piece),
        [large] * seqs,
        [flat, flat, wide, square, rows8],
        2 * work, 20 * unit, 18,
        *up_slots, *mixed_slots, conv[seqs],
    )
    back_slots = exchange_slots(back, "seq")
    grad_key, grad_value, filter_grad = call(
        functools.partial(key_body, seqs, piece, group, taps_factor),
        [struct((channels, tok), BF16)] * 2 + [struct(filter_taps.shape, F32)],
        [], 4 * unit, 10 * unit, 16,
        *back_slots, key_proj, value_proj,
    )
    if special:
        weight_grad = weight_finish(gathered, own_grad, weight_factor)
    else:
        weight_grad = weight_general(layer_input, grad_query, weight_factor)
    return (mixed_out, grad_query, grad_key, grad_value, filter_grad, weight_grad)


def solution(mesh):
    placed = (P("chan", "seq"),) * 6
    return jax.shard_map(
        per_device,
        mesh=mesh,
        in_specs=placed,
        out_specs=(P("chan", "seq"),) * 5 + (P("seq", "chan"),),
        check_vma=False,
    )
```

```python
import functools
import math

import jax
import jax.numpy as jnp
from jax import lax
from jax.experimental import pallas as pl
from jax.experimental.pallas import tpu as pltpu
from jax.sharding import PartitionSpec as P


F32 = jnp.float32
BF16 = jnp.bfloat16
EXTRA = 8
QUARTERS = 4


def vmem():
    return pl.BlockSpec(memory_space=pltpu.VMEM)


def hbm():
    return pl.BlockSpec(memory_space=pltpu.HBM)


def call(body, outs, scratch, flops, moved, limit_mib, *args, raw=0, raw_out=False, alias=None, free=0):
    many = len(outs) > 1
    return run_kernel(body, outs, scratch, flops, moved, limit_mib, many, args, raw, raw_out, alias, free)


def run_kernel(body, outs, scratch, flops, moved, limit_mib, many, args, raw, raw_out, alias, free):
    specs = [hbm()] * raw + [pl.BlockSpec(memory_space=pl.ANY)] * free
    specs += [vmem()] * (len(args) - raw - free)
    out_spec = hbm() if raw_out else vmem()
    got = pl.pallas_call(
        body,
        out_shape=tuple(outs) if many else outs[0],
        in_specs=specs,
        out_specs=tuple([out_spec] * len(outs)) if many else out_spec,
        input_output_aliases=alias or {},
        scratch_shapes=scratch,
        cost_estimate=pl.CostEstimate(
            flops=int(flops), bytes_accessed=int(moved), transcendentals=0
        ),
        compiler_params=pltpu.CompilerParams(vmem_limit_bytes=limit_mib << 20),
    )(*args)
    return got if many else (got,)


def struct(shape, dtype):
    return jax.ShapeDtypeStruct(shape, dtype)


def dot_nn(a, b):
    return lax.dot_general(a, b, (((1,), (0,)), ((), ())), preferred_element_type=F32)


def dot_nt(a, b):
    return lax.dot_general(a, b, (((1,), (1,)), ((), ())), preferred_element_type=F32)


def exchange_slots(pieces, axis):
    count = len(pieces)
    got = [pieces[0]]
    for k in range(1, count):
        pairs = [(i, i ^ k) for i in range(count)]
        got.append(lax.ppermute(pieces[k], axis, pairs))
    return got


def mixed_body(count, piece, group, key, value, taps, *refs):
    outs = refs[:count]
    key_in, value_in, taps_in, block_out, sems = refs[-5:]
    me = lax.axis_index("seq")
    row_copy = pltpu.make_async_copy(taps, taps_in, sems.at[3 * count])
    row_copy.start()
    copies = []
    for k in range(count):
        rows = pl.ds(pl.multiple_of((me ^ k) * piece, piece), piece)
        pair = (
            pltpu.make_async_copy(key.at[rows, :], key_in.at[k], sems.at[3 * k]),
            pltpu.make_async_copy(value.at[rows, :], value_in.at[k], sems.at[3 * k + 1]),
        )
        for copy in pair:
            copy.start()
        copies.append(pair)
    row_copy.wait()
    for k in range(count):
        for copy in copies[k]:
            copy.wait()
        block_out[k, 0:piece, :] = (key_in[k].astype(F32) * value_in[k].astype(F32)).astype(BF16)
        row = taps_in[pl.ds((me ^ k) * piece // group, 1), :]
        block_out[k, piece : piece + EXTRA, :] = jnp.broadcast_to(row, (EXTRA, row.shape[1])).astype(BF16)
        pltpu.make_async_copy(block_out.at[k], outs[k], sems.at[3 * k + 2]).start()
    for k in range(count):
        pltpu.make_async_copy(block_out.at[k], outs[k], sems.at[3 * k + 2]).wait()


def mixed_keep_body(count, piece, group, key, value, taps, block, *refs):
    outs, keeps = refs[:count], refs[count : count + 2]
    keep_in, keep_sems = refs[-2:]
    rows = keep_in.shape[1]
    first = (lax.axis_index("seq") & 1) * block.shape[0] // 2
    for n in range(QUARTERS):
        here = pl.ds(pl.multiple_of(first + n * rows, rows), rows)
        pltpu.make_async_copy(block.at[here, :], keep_in.at[n], keep_sems.at[2 * n]).start()
    mixed_body(count, piece, group, key, value, taps, *outs, *refs[count + 2 : -2])
    for n in range(QUARTERS):
        here = pl.ds(pl.multiple_of(first + n * rows, rows), rows)
        pltpu.make_async_copy(block.at[here, :], keep_in.at[n], keep_sems.at[2 * n]).wait()
        to = keeps[n // 2].at[n % 2, 0]
        pltpu.make_async_copy(keep_in.at[n], to, keep_sems.at[2 * n + 1]).start()
    for n in range(QUARTERS):
        to = keeps[n // 2].at[n % 2, 0]
        pltpu.make_async_copy(keep_in.at[n], to, keep_sems.at[2 * n + 1]).wait()


def upstream_body(count, piece, grad, query, *outs):
    me = lax.axis_index("seq")
    for k in range(count):
        dest = me ^ k
        rows = pl.ds(pl.multiple_of(dest * piece, piece), piece)
        outs[k][...] = (grad[rows, :].astype(F32) * query[rows, :].astype(F32)).astype(BF16)


def conv_body(count, piece, *refs):
    me = lax.axis_index("seq")
    slots = refs[:count]
    outs = refs[count : 2 * count]
    toep = refs[2 * count]
    stacked, taps, acc, before = refs[2 * count + 1 :]
    block = stacked.shape[1]
    for k in range(count):
        pos = me ^ k
        stacked[pl.ds(pl.multiple_of(pos * piece, piece), piece), :] = slots[k][0:piece, :]
        taps[pos] = slots[k][piece : piece + 8, :].astype(F32)
    row_id = lax.broadcasted_iota(jnp.int32, (block, block), 0)
    col_id = lax.broadcasted_iota(jnp.int32, (block, block), 1)
    before[...] = jnp.zeros_like(before)

    def build(n, carry):
        base = jnp.broadcast_to(taps[n][0:1, :], (block, block))
        turned = pltpu.roll(base, 0, 1, stride=1, stride_axis=0)
        toep[n] = jnp.where(col_id >= row_id, turned, before[...]).astype(BF16)
        before[...] = turned
        return carry

    lax.fori_loop(0, count, build, 0)
    acc[...] = dot_nn(stacked[...], toep[0])
    for n in range(1, count):
        rows = (count - n) * piece
        acc[n * piece :, :] += dot_nn(stacked[0:rows, :], toep[n])
    for k in range(count):
        pos = me ^ k
        outs[k][...] = acc[pl.ds(pl.multiple_of(pos * piece, piece), piece), :].astype(BF16)


def back_body(count, piece, *refs):
    me = lax.axis_index("seq")
    ups = refs[:count]
    slots = refs[count : 2 * count]
    toep = refs[2 * count]
    outs = refs[2 * count + 1 : 3 * count + 1]
    up_all, in_all, acc, before, sums = refs[3 * count + 1 :]
    block = up_all.shape[1]
    for k in range(count):
        pos = me ^ k
        rows = pl.ds(pl.multiple_of(pos * piece, piece), piece)
        up_all[rows, :] = ups[k][...]
        in_all[rows, :] = slots[k][0:piece, :]
    acc[...] = dot_nt(up_all[...], toep[0])
    for n in range(1, count):
        rows = (count - n) * piece
        acc[0:rows, :] += dot_nt(up_all[n * piece :, :], toep[n])
    row_id = lax.broadcasted_iota(jnp.int32, (block, block), 0)
    col_id = lax.broadcasted_iota(jnp.int32, (block, block), 1)
    keep = col_id + row_id >= block - 1
    top = lax.broadcasted_iota(jnp.int32, (EXTRA, block), 0) < EXTRA // 2
    flip = (col_id + row_id == block - 1).astype(BF16)
    turned_in = dot_nt(flip, in_all[...]).astype(BF16)
    before[...] = jnp.zeros_like(before)
    for n in reversed(range(count)):
        rows = (count - n) * piece
        prod = dot_nn(turned_in[:, 0:rows], up_all[n * piece :, :])
        both = jnp.where(keep, prod, before[...])
        before[...] = prod
        lined = pltpu.roll(both, 1, 1, stride=1, stride_axis=0)
        total = jnp.sum(lined, axis=0, keepdims=True)
        sums[n] = jnp.broadcast_to(total, (8, block))
    for k in range(count):
        pos = me ^ k
        outs[k][0:piece, :] = acc[pl.ds(pl.multiple_of(pos * piece, piece), piece), :].astype(BF16)
        full = sums[pos]
        high = full.astype(BF16)
        low = full - high.astype(F32)
        outs[k][piece : piece + EXTRA, :] = jnp.where(top, high.astype(F32), low).astype(BF16)


def query_body(count, piece, *refs):
    me = lax.axis_index("seq")
    slots = refs[:count]
    query, grad, mixed, grad_query, again = refs[count:]
    for k in range(count):
        pos = me ^ k
        rows = pl.ds(pl.multiple_of(pos * piece, piece), piece)
        conv = slots[k][...].astype(F32)
        mixed[rows, :] = (query[rows, :].astype(F32) * conv).astype(BF16)
        value = (grad[rows, :].astype(F32) * conv).astype(BF16)
        grad_query[rows, :] = value
        again[rows, :] = value


def key_body(count, piece, group, factor, *refs):
    me = lax.axis_index("seq")
    slots = refs[:count]
    key, value, grad_key, grad_value, taps_grad = refs[count:]
    row_id = lax.broadcasted_iota(jnp.int32, taps_grad.shape, 0)
    total = jnp.zeros(taps_grad.shape, F32)
    for k in range(count):
        pos = me ^ k
        rows = pl.ds(pl.multiple_of(pos * piece, piece), piece)
        back = slots[k][0:piece, :].astype(F32)
        grad_key[rows, :] = (back * value[rows, :].astype(F32)).astype(BF16)
        grad_value[rows, :] = (back * key[rows, :].astype(F32)).astype(BF16)
        tail = slots[k][piece : piece + EXTRA, :].astype(F32)
        row = tail[0:1, :] + tail[EXTRA // 2 : EXTRA // 2 + 1, :]
        total = total + jnp.where(row_id == pos * piece // group, row, 0.0)
    taps_grad[...] = total * factor


def stack_body(kept_x, kept_y, other, *refs):
    del kept_x, kept_y
    outs, sems = refs[:-1], refs[-1]
    rows = outs[0].shape[2]
    first = (lax.axis_index("seq") & 1) * other.shape[0] // 2
    copies = []
    for n in range(QUARTERS):
        here = pl.ds(pl.multiple_of(first + n * rows, rows), rows)
        to = outs[n // 2].at[n % 2, 1]
        copies.append(pltpu.make_async_copy(other.at[here, :], to, sems.at[n]))
    for copy in copies:
        copy.start()
    for copy in copies:
        copy.wait()


def is_inner():
    plane = lax.axis_index("chan")
    return (plane == 1) | (plane == 2)


def both_products(stack, own_grad, other_grad):
    return dot_nt(stack[0], own_grad[...]) + dot_nt(stack[1], other_grad[...])


def early_body(start, own, a1, a2, b2, own_grad, other_grad, total, stack):
    rows = total.shape[1]
    unit = own.shape[2]
    inner = is_inner()

    def place(source, d):
        for n in range(rows // unit):
            at = d * rows + n * unit
            for side in range(2):
                stack[side, at : at + unit, :] = source[start + n, side]

    place(own, 0)
    place(a1, 1)

    @pl.when(inner)
    def _():
        place(b2, 2)

    @pl.when(jnp.logical_not(inner))
    def _():
        place(a2, 2)

    full = both_products(stack, own_grad, other_grad)
    for d in range(3):
        total[d] = full[d * rows : (d + 1) * rows, :]


def weight_body(start, last, a3, b1, own_grad, other_grad, total, *refs):
    mine, send_p, send_q, keep_p, keep_q, stack, final = refs
    rows = mine.shape[0]
    unit = b1.shape[2]
    half = mine.shape[1] // 2
    inner = is_inner()
    turn = (lax.axis_index("seq") >> 1) ^ lax.axis_index("chan")

    def place(source, offset):
        for n in range(rows // unit):
            for side in range(2):
                stack[side, n * unit : (n + 1) * unit, :] = source[start + n - offset, side]

    @pl.when(inner)
    def _():
        place(b1, 0)

    @pl.when(jnp.logical_not(inner))
    def _():
        place(a3, last)

    def emit(r, block):
        left, right = slice(0, half), slice(half, 2 * half)
        if r == 0:
            mine[...] = block[...]
        elif r == 1:
            send_p[0] = block[:, left].astype(BF16)
            keep_q[...] = block[:, right]
        elif r == 2:
            send_q[0] = block[:, right].astype(BF16)
            keep_p[...] = block[:, left]
        else:
            send_p[1] = block[:, left].astype(BF16)
            send_q[1] = block[:, right].astype(BF16)

    final[...] = both_products(stack, own_grad, other_grad)
    for d in range(4):
        for r in range(4):

            @pl.when(turn == (d ^ r))
            def _(d=d, r=r):
                emit(r, final if d == 3 else total.at[d])


def middle_body(keep_p, got_p, keep_q, got_q, out_p, out_q):
    out_p[...] = (keep_p[...] + got_p[1].astype(F32)).astype(BF16)
    out_q[...] = (keep_q[...] + got_q[1].astype(F32)).astype(BF16)


def finish_body(chunks, begin, factor, *refs):
    out, block, sem = refs[-3:]
    half = refs[0].shape[1] // 2
    first = 0
    for n in range(chunks):
        mine, got_p, got_q, last_p, last_q = refs[5 * n : 5 * n + 5]
        here = slice(first, first + mine.shape[0])
        first += mine.shape[0]
        left = mine[:, :half] + got_p[0].astype(F32) + last_p[...].astype(F32)
        right = mine[:, half:] + got_q[0].astype(F32) + last_q[...].astype(F32)
        block[here, :half] = left * factor
        block[here, half:] = right * factor
    copy = pltpu.make_async_copy(block, out.at[pl.ds(begin, first), :], sem)
    copy.start()
    copy.wait()


def last_body(chunks, begin, factor, whole, *refs):
    del whole
    finish_body(chunks, begin, factor, *refs)


def plane_pairs(seqs, chans):
    outer = [(i, i ^ 1) for i in range(chans)]
    middle = []
    for i in range(seqs):
        for j in range(chans):
            to = (i, j ^ 3) if j in (1, 2) else (i ^ 1, j)
            middle.append((i * chans + j, to[0] * chans + to[1]))
    return outer, middle


def weight_start(other, kept):
    seqs, chans = lax.axis_size("seq"), lax.axis_size("chan")
    quarter = struct(kept[0].shape, BF16)
    own = call(
        stack_body, [quarter] * 2, [pltpu.SemaphoreType.DMA((QUARTERS,))],
        other.size, 2 * other.size, 8,
        *kept, other, raw=2, free=1, raw_out=True, alias={0: 0, 1: 1},
    )
    outer, middle = plane_pairs(seqs, chans)
    both = ("seq", "chan")
    a1x = lax.ppermute(own[0], "chan", outer)
    b1x = lax.ppermute(own[0], both, middle)
    a1y = lax.ppermute(own[1], "chan", outer)
    b1y = lax.ppermute(own[1], both, middle)
    a2x = lax.ppermute(b1x, "chan", outer)
    b2x = lax.ppermute(a1x, both, middle)
    a3x = lax.ppermute(b2x, "chan", outer)
    a2y = lax.ppermute(b1y, "chan", outer)
    b2y = lax.ppermute(a1y, both, middle)
    a3y = lax.ppermute(b2y[0:1], "chan", outer)
    a3z = lax.ppermute(b2y[1:2], "chan", outer)
    return [
        (0, 2, 0, (own[0], a1x, a2x, a3x, b1x, b2x)),
        (0, 1, 0, (own[1], a1y, a2y, a3y, b1y, b2y)),
        (1, 1, 1, (own[1], a1y, a2y, a3z, b1y, b2y)),
    ]


def weight_finish(gathered, grad_query, factor):
    seqs = lax.axis_size("seq")
    outputs, tok = grad_query.shape
    half = outputs // 2
    swap = [(i, i ^ 1) for i in range(seqs)]
    along = [(i, i ^ 2) for i in range(seqs)]
    across = [(i, i ^ 4) for i in range(seqs)]
    other_grad = lax.ppermute(grad_query, "seq", swap)
    parts = []
    for start, count, last, sources in gathered:
        rows = count * sources[0].shape[2]
        own, a1, a2, a3, b1, b2 = sources
        (total,) = call(
            functools.partial(early_body, start),
            [struct((3, rows, outputs), F32)],
            [pltpu.VMEM((2, 3 * rows, tok), BF16)],
            12 * rows * outputs * tok, 8 << 20, 16,
            own, a1, a2, b2, grad_query, other_grad,
        )
        mine, send_p, send_q, keep_p, keep_q = call(
            functools.partial(weight_body, start, last),
            [
                struct((rows, outputs), F32),
                struct((2, rows, half), BF16),
                struct((2, rows, half), BF16),
                struct((rows, half), F32),
                struct((rows, half), F32),
            ],
            [pltpu.VMEM((2, rows, tok), BF16), pltpu.VMEM((rows, outputs), F32)],
            4 * rows * outputs * tok, 8 << 20, 16,
            a3, b1, grad_query, other_grad, total,
        )
        got_p = lax.ppermute(send_p, "seq", along)
        got_q = lax.ppermute(send_q, "seq", across)
        next_p, next_q = call(
            middle_body,
            [struct((rows, half), BF16)] * 2,
            [],
            rows * outputs,
            4 << 20,
            8,
            keep_p,
            got_p,
            keep_q,
            got_q,
        )
        last_p = lax.ppermute(next_p, "seq", across)
        last_q = lax.ppermute(next_q, "seq", along)
        parts += [mine, got_p, got_q, last_p, last_q]
    total = QUARTERS * gathered[0][3][0].shape[2]
    result = struct((total, outputs), F32)
    early = total - parts[-5].shape[0]
    (out,) = call(
        functools.partial(finish_body, len(gathered) - 1, 0, factor),
        [result], [pltpu.VMEM((early, outputs), F32), pltpu.SemaphoreType.DMA],
        3 * early * outputs, 8 * early * outputs, 12,
        *parts[:-5], raw_out=True,
    )
    (out,) = call(
        functools.partial(last_body, 1, early, factor),
        [result], [pltpu.VMEM((total - early, outputs), F32), pltpu.SemaphoreType.DMA],
        3 * outputs * (total - early), 8 * outputs * (total - early), 8,
        out, *parts[-5:], raw=1, raw_out=True, alias={0: 0},
    )
    return out


def weight_general(layer_input, grad_query, factor):
    gathered = lax.all_gather(layer_input, "chan", axis=0, tiled=True)
    summed = lax.psum_scatter(
        jnp.einsum("it,jt->ij", gathered, grad_query, preferred_element_type=F32),
        "seq",
        scatter_dimension=0,
        tiled=True,
    )
    return summed * factor


def per_device(layer_input, query_proj, key_proj, value_proj, filter_taps, grad_out):
    seqs = lax.axis_size("seq")
    chans = lax.axis_size("chan")
    channels, tok = query_proj.shape
    length = seqs * tok
    piece = channels // seqs
    group = channels // filter_taps.shape[0]
    weight_factor = 1.0 / math.sqrt(length)
    taps_factor = 1.0 / math.sqrt(group * length)
    special = seqs == 8 and chans == 4
    small = struct((piece, tok), BF16)
    large = struct((piece + EXTRA, tok), BF16)
    flat = pltpu.VMEM((channels, tok), BF16)
    wide = pltpu.VMEM((channels, tok), F32)
    square = pltpu.VMEM((tok, tok), F32)
    rows8 = pltpu.VMEM((seqs, 8, tok), F32)
    unit = channels * tok
    work = unit * tok * (seqs + 1)

    buffers = [
        pltpu.VMEM((seqs, piece, tok), BF16),
        pltpu.VMEM((seqs, piece, tok), BF16),
        pltpu.VMEM(filter_taps.shape, F32),
        pltpu.VMEM((seqs, piece + EXTRA, tok), BF16),
        pltpu.SemaphoreType.DMA((3 * seqs + 1,)),
    ]
    first_args = (key_proj, value_proj, filter_taps)
    if special:
        other = lax.ppermute(layer_input, "seq", [(i, i ^ 1) for i in range(seqs)])
        rows = channels // 2 // QUARTERS
        first = call(
            functools.partial(mixed_keep_body, seqs, piece, group),
            [large] * seqs + [struct((QUARTERS // 2, 2, rows, tok), BF16)] * 2,
            buffers + [pltpu.VMEM((QUARTERS, rows, tok), BF16), pltpu.SemaphoreType.DMA((2 * QUARTERS,))],
            3 * unit, 8 * unit, 58,
            *first_args, layer_input, raw=4, raw_out=True,
        )
        mixed, kept = first[:seqs], first[seqs:]
    else:
        mixed = call(
            functools.partial(mixed_body, seqs, piece, group),
            [large] * seqs, buffers, 3 * unit, 6 * unit, 58,
            *first_args, raw=3, raw_out=True,
        )
    mixed_slots = exchange_slots(mixed, "seq")
    upstream = call(
        functools.partial(upstream_body, seqs, piece),
        [small] * seqs, [], 3 * unit, 6 * unit, 16,
        grad_out, query_proj,
    )
    up_slots = exchange_slots(upstream, "seq")
    if special:
        gathered = weight_start(other, kept)
    conv = call(
        functools.partial(conv_body, seqs, piece),
        [small] * seqs + [struct((seqs, tok, tok), BF16)],
        [flat, rows8, wide, square],
        work, 16 * unit, 14,
        *mixed_slots,
    )
    conv_slots = exchange_slots(conv[:seqs], "seq")
    mixed_out, grad_query, own_grad = call(
        functools.partial(query_body, seqs, piece),
        [struct((channels, tok), BF16)] * 3, [], 4 * unit, 10 * unit, 16,
        *conv_slots, query_proj, grad_out,
    )
    back = call(
        functools.partial(back_body, seqs, piece),
        [large] * seqs,
        [flat, flat, wide, square, rows8],
        2 * work, 20 * unit, 18,
        *up_slots, *mixed_slots, conv[seqs],
    )
    back_slots = exchange_slots(back, "seq")
    grad_key, grad_value, filter_grad = call(
        functools.partial(key_body, seqs, piece, group, taps_factor),
        [struct((channels, tok), BF16)] * 2 + [struct(filter_taps.shape, F32)],
        [], 4 * unit, 10 * unit, 16,
        *back_slots, key_proj, value_proj,
    )
    if special:
        weight_grad = weight_finish(gathered, own_grad, weight_factor)
    else:
        weight_grad = weight_general(layer_input, grad_query, weight_factor)
    return (mixed_out, grad_query, grad_key, grad_value, filter_grad, weight_grad)


def solution(mesh):
    placed = (P("chan", "seq"),) * 6
    return jax.shard_map(
        per_device,
        mesh=mesh,
        in_specs=placed,
        out_specs=(P("chan", "seq"),) * 5 + (P("seq", "chan"),),
        check_vma=False,
    )
```
